32 devices in a mesh: bucket: 8 (over y, x, core), rep: 4 (over z).
Axes of the slice: x: 2, y: 2, z: 4, core: 2. Of those that a mesh axis runs over, the one named last changes fastest.
Arguments:
- src_table: float32 [16384, 256], P(('bucket', 'rep')), may hold values from -6 to 6
- src_state: float32 [16384], P(('bucket', 'rep')), may hold values from 0.05 to 0.5
- dst_table: float32 [4096, 256], P(('bucket', 'rep')), may hold values from -6 to 6
- dst_state: float32 [4096], P(('bucket', 'rep')), may hold values from 0.05 to 0.5
- rel_table: float32 [64, 256], replicated, may hold values from 0.25 to 1.75
- partners: int32 [2, 8], replicated, may hold values from 0 to 7, as said below
- tiles: int32 [8, 4, 2, 64], P('bucket', 'rep'), may hold values from 0 to 15
- tile_rel: int32 [8, 4, 2, 64], P('bucket', 'rep'), may hold values from 0 to 63
- counts: int32 [8, 4, 2], P('bucket', 'rep'), may hold values from 1 to 64, as said below
Outputs:
- src_out: float32 [16384, 256], P(('bucket', 'rep'))
- src_state_out: float32 [16384], P(('bucket', 'rep'))
- dst_out: float32 [4096, 256], P(('bucket', 'rep'))
- dst_state_out: float32 [4096], P(('bucket', 'rep'))
The draws below stay inside these ranges and needn't reach their ends.
Inputs may be any that keep to these rules, and one draw needn't show every extreme that they name: partners[k, b] = b XOR m_k for one mask m_k of round k, 1 to 7, a different mask in each round. Only the first counts[b, r, k] slots of a device's round are live; some device holds 64 live tiles in every draw.
All inputs are finite; a program needn't handle non-finite values.
Results may differ from the reference program's by a relative error of at most 0.002.
Values may be sent and summed in bfloat16 or wider, within the bound.
No kernel may reach another device: no remote copies, remote signals or barrier semaphores. Data moves between devices by JAX's collectives and lax.ppermute only.
A program may use at most 64 MiB of HBM per device.

```python
import math
import jax
import jax.numpy as jnp
from jax import lax

D = 256
TILE = 128
ROUNDS = 2
REL = 64
SRC_DEV = 512
MAXT = 64
PART = 512
ENT_SRC = 16384
ENT_DST = 4096
N_BUCKET = 8
N_REP = 4


def draw_partners(key, part):
    order = jax.random.permutation(jax.random.fold_in(key, 21), N_BUCKET - 1) + 1
    masks = order[:ROUNDS].astype(jnp.int32)
    buckets = jnp.arange(N_BUCKET, dtype=jnp.int32)
    return jnp.bitwise_xor(buckets[None, :], masks[:, None]).astype(jnp.int32)


def draw_counts(key, part):
    shape = (N_BUCKET, N_REP, ROUNDS)
    base = jax.random.randint(jax.random.fold_in(key, 11), shape, 1, MAXT // 2 + 1)
    filled = jax.random.randint(jax.random.fold_in(key, 12), shape, 0, 8) == 0
    values = jnp.where(filled, MAXT, base).reshape(-1)
    where_full = jax.random.randint(jax.random.fold_in(key, 13), (), 0, values.shape[0])
    values = values.at[where_full].set(MAXT)
    return values.reshape(shape).astype(jnp.int32)


def touch_ends(values, rng, least, high):
    index_at = [jax.random.randint(jax.random.fold_in(rng, axis), (), 0, length) for axis, length in enumerate(values.shape)]
    main_axis = values.shape.index(max(values.shape))
    beside = index_at[:main_axis] + [(index_at[main_axis] + 1) % values.shape[main_axis]] + index_at[main_axis + 1:]
    return values.at[tuple(index_at)].set(least).at[tuple(beside)].set(high)


def block_levels(stream_key, dims, shards, low, high):
    level, own = 1.0, jax.random.fold_in(stream_key, 6)
    for position, parts in shards:
        heights = jnp.exp(jax.random.uniform(jax.random.fold_in(own, position), (parts,), jnp.float32, low / len(shards), high / len(shards)))
        level = level * jnp.repeat(heights, dims[position] // parts).reshape([-1 if axis == position else 1 for axis in range(len(dims))])
    return level


def centred(own_key, shape, width, most, pieces=(), kind=jnp.bfloat16):
    loudness = block_levels(own_key, shape, pieces, -0.22, 0.18) if pieces else 1.0
    drawn = jax.random.normal(own_key, shape, jnp.float32) * width * loudness
    return jnp.minimum(jnp.maximum(drawn, -most), most).astype(kind)


def setup_inputs(seed: int = 0) -> dict:
    key_of = jax.random.split(jax.random.key(seed), 10)
    src_table = centred(key_of[0], (ENT_SRC, D), 1.0, 6.0, ((0, 32),), jnp.float32)
    src_state = jnp.clip(jnp.exp(math.log(0.5) - 2.3025851 * jax.random.uniform(key_of[1], (ENT_SRC,), jnp.float32) ** block_levels(key_of[1], (ENT_SRC,), ((0, 32),), -0.2, 0.2)), 0.05, 0.5)
    dst_table = centred(key_of[2], (ENT_DST, D), 1.0, 6.0, ((0, 32),), jnp.float32)
    dst_state = jnp.clip(jnp.exp(math.log(0.5) - 2.3025851 * jax.random.uniform(key_of[3], (ENT_DST,), jnp.float32) ** block_levels(key_of[3], (ENT_DST,), ((0, 32),), -0.2, 0.2)), 0.05, 0.5)
    rel_table = jnp.clip(jax.random.uniform(key_of[4], (REL, D), jnp.float32, 0.25, 1.75), 0.25, 1.75)
    partners = draw_partners(jax.random.fold_in(key_of[9], 71), 0)
    tiles = touch_ends(jax.random.randint(key_of[6], (N_BUCKET, N_REP, ROUNDS, MAXT), 0, SRC_DEV // TILE * (PART // TILE)), jax.random.fold_in(key_of[6], 1), 0, (SRC_DEV // TILE * (PART // TILE)) - 1).astype(jnp.int32)
    tile_rel = touch_ends(jax.random.randint(key_of[7], (N_BUCKET, N_REP, ROUNDS, MAXT), 0, REL), jax.random.fold_in(key_of[7], 1), 0, REL - 1).astype(jnp.int32)
    counts = draw_counts(jax.random.fold_in(key_of[9], 71), 0)
    return dict(src_table=src_table, src_state=src_state, dst_table=dst_table, dst_state=dst_state, rel_table=rel_table, partners=partners, tiles=tiles, tile_rel=tile_rel, counts=counts)


learn_rate = 0.1

def tile_terms(src_blocks, dst_blocks, tile_list, rel_list, live_count, rel_table):
    dst_number = dst_blocks.shape[0]
    src_number = src_blocks.shape[0]
    score_scale = D ** (-0.5)
    src_index = (tile_list // dst_number).astype(jnp.int32)
    dst_index = (tile_list % dst_number).astype(jnp.int32)
    rel_pick = rel_table[rel_list.astype(jnp.int32)]
    src_pick = src_blocks[src_index].astype(jnp.float32)
    dst_pick = dst_blocks[dst_index].astype(jnp.float32)
    src_rel = (src_pick * rel_pick[:, None, :]).astype(jnp.bfloat16)
    src_rel = lax.optimization_barrier(src_rel).astype(jnp.float32)
    scores = jnp.einsum('tnd,tmd->tnm', src_rel, dst_pick, precision=lax.Precision.HIGHEST) * score_scale
    live_tiles = (jnp.arange(MAXT, dtype=jnp.int32) < live_count).astype(jnp.float32)
    diagonal_ones = jnp.eye(TILE, dtype=jnp.float32)
    slope = ((jax.nn.sigmoid(scores) - diagonal_ones) * live_tiles[:, None, None]).astype(jnp.bfloat16)
    slope = lax.optimization_barrier(slope).astype(jnp.float32)
    src_terms = jnp.einsum('tnm,tmd->tnd', slope, dst_pick, precision=lax.Precision.HIGHEST) * rel_pick[:, None, :] * score_scale
    dst_terms = jnp.einsum('tnm,tnd->tmd', slope, src_rel, precision=lax.Precision.HIGHEST) * score_scale
    src_onehot = (src_index[:, None] == jnp.arange(src_number, dtype=jnp.int32)[None, :]).astype(jnp.float32)
    dst_onehot = (dst_index[:, None] == jnp.arange(dst_number, dtype=jnp.int32)[None, :]).astype(jnp.float32)
    src_grad = jnp.einsum('ts,tnd->snd', src_onehot, src_terms, precision=lax.Precision.HIGHEST)
    dst_grad = jnp.einsum('ts,tnd->snd', dst_onehot, dst_terms, precision=lax.Precision.HIGHEST)
    return (src_grad.reshape(-1, D), dst_grad.reshape(-1, D))

def adagrad(embedding, accumulator, gradient):
    accumulator = accumulator + lax.optimization_barrier(jnp.mean(gradient * gradient, axis=1))
    embedding = embedding - learn_rate * gradient / jnp.sqrt(accumulator)[:, None]
    return (embedding, accumulator)

def reference(src_table, src_state, dst_table, dst_state, rel_table, partners, tiles, tile_rel, counts):
    for round_index in range(ROUNDS):
        src_low = src_table.astype(jnp.bfloat16).reshape(N_BUCKET, N_REP, SRC_DEV // TILE, TILE, D)
        dst_low = dst_table.astype(jnp.bfloat16).reshape(N_BUCKET, PART // TILE, TILE, D)
        partner_row = partners[round_index]

        def one_bucket(inputs):
            src_bucket, partner_bucket, tiles_bucket, rel_bucket, counts_bucket = inputs
            dst_bucket = dst_low[partner_bucket]
            src_grad, dst_part = jax.vmap(tile_terms, in_axes=(0, None, 0, 0, 0, None))(src_bucket, dst_bucket, tiles_bucket, rel_bucket, counts_bucket, rel_table)
            dst_part = lax.optimization_barrier(dst_part.astype(jnp.bfloat16)).astype(jnp.float32)
            return (src_grad, lax.optimization_barrier(jnp.sum(dst_part, axis=0)).astype(jnp.bfloat16))
        src_grad, dst_sum = lax.map(one_bucket, (src_low, partner_row, tiles[:, :, round_index], tile_rel[:, :, round_index], counts[:, :, round_index]))
        dst_grad = dst_sum[partner_row].astype(jnp.float32).reshape(-1, D)
        src_table, src_state = adagrad(src_table, src_state, src_grad.reshape(-1, D))
        dst_table, dst_state = adagrad(dst_table, dst_state, dst_grad)
    return (src_table, src_state, dst_table, dst_state)
```

```python
import functools

import jax
import jax.numpy as jnp
from jax import lax
from jax.experimental import pallas as pl
from jax.experimental.pallas import tpu as pltpu
from jax.sharding import PartitionSpec as P

TILE = 128
GROUP = 4
LOW_BITS = 3

learn_rate = 0.1

AXES = ("bucket", "rep")
SMEM = pl.BlockSpec(memory_space=pltpu.SMEM)
VMEM = pl.BlockSpec(memory_space=pltpu.VMEM)


def send(array, bucket_xor, rep_xor):
    if bucket_xor == 0 and rep_xor == 0:
        return array
    buckets, reps = lax.axis_size("bucket"), lax.axis_size("rep")
    pairs = [
        (b * reps + r, (b ^ bucket_xor) * reps + (r ^ rep_xor))
        for b in range(buckets)
        for r in range(reps)
    ]
    return lax.ppermute(array, AXES, pairs)


def bit_chunks():
    bits = lax.axis_size("bucket").bit_length() - 1
    return [(at, min(LOW_BITS, bits - at)) for at in range(0, bits, LOW_BITS)]


def by_mask(mask, chunk, branch, *operands):
    first, width = chunk
    buckets = lax.axis_size("bucket")
    least = 1 if (1 << width) == buckets else 0
    index = jnp.bitwise_and(jnp.right_shift(mask, first), (1 << width) - 1) - least
    branches = [functools.partial(branch, value << first) for value in range(least, 1 << width)]
    return lax.switch(index, branches, *operands)


def spread(rows, mask):
    low, *high = bit_chunks()
    for chunk in high:
        rows = by_mask(mask, chunk, lambda value, x: send(x, value, 0), rows)

    def direct(value, x):
        return tuple(send(x, value, j) for j in range(lax.axis_size("rep")))

    return by_mask(mask, low, direct, rows)


def collect(parts, mask):
    low, *high = bit_chunks()

    def direct(value, *xs):
        return tuple(send(x, value, j) for j, x in enumerate(xs))

    got = by_mask(mask, low, direct, *parts)
    total = got[0].astype(jnp.float32)
    for x in got[1:]:
        total = total + x.astype(jnp.float32)
    total = total.astype(jnp.bfloat16)
    for chunk in high:
        total = by_mask(mask, chunk, lambda value, x: send(x, value, 0), total)
    return total.astype(jnp.float32)


def prep_kernel(dst_number, shard_blocks, none_rel, rep, tiles, rel, counts, src_of, rel_of, dst_of, steps):
    rounds = tiles.shape[0]
    me = rep[0]

    def key(code):
        e = lax.rem(code, dst_number)
        return jnp.bitwise_xor(e // shard_blocks, me) * shard_blocks + lax.rem(e, shard_blocks)

    for k in range(rounds):
        live = counts[k]

        def count(t, c):
            e = key(tiles[k, t])
            return tuple(c[i] + jnp.where(e == i, 1, 0) for i in range(dst_number))

        number = lax.fori_loop(0, live, count, (jnp.int32(0),) * dst_number)
        starts = [jnp.int32(0)]
        for i in range(dst_number):
            starts.append(starts[-1] + ((number[i] + GROUP - 1) // GROUP) * GROUP)
        steps[k] = starts[-1] // GROUP

        def place(t, at):
            code = tiles[k, t]
            e = key(code)
            p = at[0]
            for i in range(1, dst_number):
                p = jnp.where(e == i, at[i], p)
            src_of[k, p] = code // dst_number
            rel_of[k, p] = rel[k, t]
            return tuple(at[i] + jnp.where(e == i, 1, 0) for i in range(dst_number))

        ends = lax.fori_loop(0, live, place, tuple(starts[:-1]))
        for i in range(dst_number):

            def pad(p, carry):
                src_of[k, p] = 0
                rel_of[k, p] = none_rel
                return carry

            lax.fori_loop(ends[i], starts[i + 1], pad, 0)

            def name(q, carry, i=i):
                dst_of[k, q] = jnp.int32(i)
                return carry

            lax.fori_loop(starts[i] // GROUP, starts[i + 1] // GROUP, name, 0)


def prep(tiles, rel, counts, dst_number, shard_blocks, none_rel):
    rounds, slots = tiles.shape
    length = -(-(slots + dst_number * GROUP) // GROUP) * GROUP
    rep = lax.axis_index("rep").astype(jnp.int32).reshape(1)
    return pl.pallas_call(
        functools.partial(prep_kernel, dst_number, shard_blocks, none_rel),
        in_specs=[SMEM] * 4,
        out_specs=[SMEM] * 4,
        out_shape=[
            jax.ShapeDtypeStruct((rounds, length), jnp.int32),
            jax.ShapeDtypeStruct((rounds, length), jnp.int32),
            jax.ShapeDtypeStruct((rounds, length // GROUP), jnp.int32),
            jax.ShapeDtypeStruct((rounds,), jnp.int32),
        ],
        name="sort_tiles",
    )(rep, tiles, rel, counts)


def tile_kernel(round_index, reps, src_of, rel_of, dst_of, steps, src_ref, rel_ref, *refs):
    blocks, src_grad, parts = refs[:reps], refs[reps], refs[reps + 1 : 2 * reps + 1]
    src_low, dst_all, dst_grad = refs[2 * reps + 1 :]
    shard = blocks[0].shape[0]
    src_low[...] = src_ref[...].astype(jnp.bfloat16).astype(jnp.float32)
    for j in range(reps):
        dst_all[pl.ds(j * shard, shard), :] = blocks[j][...]
    src_grad[...] = jnp.zeros_like(src_grad)
    dst_grad[...] = jnp.zeros_like(dst_grad)
    row_id = lax.broadcasted_iota(jnp.int32, (TILE, TILE), 0)
    column_id = lax.broadcasted_iota(jnp.int32, (TILE, TILE), 1)
    offset = jnp.where(row_id == column_id, -1.0, 1.0).astype(jnp.float32)

    def step(q, carry):
        at = pl.multiple_of(dst_of[round_index, q] * TILE, TILE)
        dst = dst_all[pl.ds(at, TILE), :]
        where, rows, low = [], [], []
        for g in range(GROUP):
            s = pl.multiple_of(src_of[round_index, q * GROUP + g] * TILE, TILE)
            row = rel_ref[pl.ds(rel_of[round_index, q * GROUP + g], 1), :]
            where.append(s)
            rows.append(row)
            low.append((src_low[pl.ds(s, TILE), :] * row).astype(jnp.bfloat16))
        src_rel = jnp.concatenate(low, 0)
        scores = lax.dot_general(
            src_rel, dst, (((1,), (1,)), ((), ())), preferred_element_type=jnp.float32
        )
        slope = jnp.concatenate(
            [
                (jnp.tanh(scores[g * TILE : (g + 1) * TILE]) + offset).astype(jnp.bfloat16)
                for g in range(GROUP)
            ],
            0,
        )
        src_terms = jnp.dot(slope, dst, preferred_element_type=jnp.float32)
        dst_terms = lax.dot_general(
            slope, src_rel, (((0,), (0,)), ((), ())), preferred_element_type=jnp.float32
        )
        for g in range(GROUP):
            src_grad[pl.ds(where[g], TILE), :] += src_terms[g * TILE : (g + 1) * TILE] * rows[g]
        dst_grad[pl.ds(at, TILE), :] += dst_terms
        return carry

    lax.fori_loop(0, steps[round_index], step, 0)
    for j in range(reps):
        parts[j][...] = dst_grad[pl.ds(j * shard, shard), :].astype(jnp.bfloat16)


def tile_work(round_index, lists, src_table, rel_rows, blocks):
    reps = len(blocks)
    shard, width = blocks[0].shape
    slots = lists[0].shape[1]
    flops = 6 * slots * TILE * TILE * width
    src_grad, *parts = pl.pallas_call(
        functools.partial(tile_kernel, round_index, reps),
        in_specs=[SMEM] * 4 + [VMEM] * (2 + reps),
        out_specs=[VMEM] * (1 + reps),
        out_shape=[jax.ShapeDtypeStruct(src_table.shape, jnp.float32)]
        + [jax.ShapeDtypeStruct((shard, width), jnp.bfloat16)] * reps,
        scratch_shapes=[
            pltpu.VMEM(src_table.shape, jnp.float32),
            pltpu.VMEM((reps * shard, width), jnp.bfloat16),
            pltpu.VMEM((reps * shard, width), jnp.float32),
        ],
        cost_estimate=pl.CostEstimate(
            flops=flops, bytes_accessed=8 * src_table.size, transcendentals=slots * TILE * TILE
        ),
        name="tile_work",
    )(*lists, src_table, rel_rows, *blocks)
    return src_grad, parts


def adagrad(embedding, accumulator, gradient):
    accumulator = accumulator + jnp.mean(gradient * gradient, axis=1)
    embedding = embedding - learn_rate * gradient / jnp.sqrt(accumulator)[:, None]
    return (embedding, accumulator)


def per_device(
    src_table, src_state, dst_table, dst_state, rel_table, partners, tiles, tile_rel, counts
):
    reps = lax.axis_size("rep")
    width = src_table.shape[1]
    rounds = partners.shape[0]
    shard_blocks = dst_table.shape[0] // TILE
    rel_rows = jnp.concatenate(
        [rel_table * (0.5 * width**-0.5), jnp.zeros((8, width), jnp.float32)], 0
    )
    lists = prep(
        tiles[0, 0], tile_rel[0, 0], counts[0, 0], reps * shard_blocks, shard_blocks, rel_table.shape[0]
    )
    for k in range(rounds):
        mask = partners[k, 0]
        blocks = spread(dst_table.astype(jnp.bfloat16), mask)
        src_grad, parts = tile_work(k, lists, src_table, rel_rows, blocks)
        dst_grad = collect(parts, mask)
        src_table, src_state = adagrad(src_table, src_state, src_grad)
        dst_table, dst_state = adagrad(dst_table, dst_state, dst_grad)
    return (src_table, src_state, dst_table, dst_state)


def solution(mesh):
    table, state = P(AXES, None), P(AXES)
    in_specs = (
        table,
        state,
        table,
        state,
        P(),
        P(),
        P("bucket", "rep", None, None),
        P("bucket", "rep", None, None),
        P("bucket", "rep", None),
    )
    return jax.shard_map(
        per_device,
        mesh=mesh,
        in_specs=in_specs,
        out_specs=(table, state, table, state),
        check_vma=False,
    )
```

```python
import functools

import jax
import jax.numpy as jnp
from jax import lax
from jax.experimental import pallas as pl
from jax.experimental.pallas import tpu as pltpu
from jax.sharding import PartitionSpec as P

TILE = 128
GROUP = 4
LOW_BITS = 3
PIECES = 4

learn_rate = 0.1

AXES = ("bucket", "rep")
SMEM = pl.BlockSpec(memory_space=pltpu.SMEM)
VMEM = pl.BlockSpec(memory_space=pltpu.VMEM)
GRANT = pltpu.CompilerParams(vmem_limit_bytes=12 * 1024 * 1024)


def send(array, bucket_xor, rep_xor):
    if bucket_xor == 0 and rep_xor == 0:
        return array
    buckets, reps = lax.axis_size("bucket"), lax.axis_size("rep")
    pairs = [
        (b * reps + r, (b ^ bucket_xor) * reps + (r ^ rep_xor))
        for b in range(buckets)
        for r in range(reps)
    ]
    return lax.ppermute(array, AXES, pairs)


def bit_chunks():
    bits = lax.axis_size("bucket").bit_length() - 1
    return [(at, min(LOW_BITS, bits - at)) for at in range(0, bits, LOW_BITS)]


def by_mask(mask, chunk, branch, operands):
    first, width = chunk
    least = 1 if (1 << width) == lax.axis_size("bucket") else 0
    index = jnp.bitwise_and(jnp.right_shift(mask, first), (1 << width) - 1) - least
    branches = [functools.partial(branch, value << first) for value in range(least, 1 << width)]
    return lax.switch(index, branches, operands)


def send_high(rows, mask):
    for chunk in bit_chunks()[1:]:
        rows = by_mask(mask, chunk, lambda value, x: send(x, value, 0), rows)
    return rows


def prep_kernel(reps, shard_blocks, rep, tiles, rel, counts, src_ref, rel_ref, plan, low_ref, row_ref):
    rounds, slots = tiles.shape
    number = reps * shard_blocks
    none_rel = rel_ref.shape[0]
    me = rep[0]

    def key(code):
        e = lax.rem(code, number)
        return jnp.bitwise_xor(e // shard_blocks, me) * shard_blocks + lax.rem(e, shard_blocks)

    low_ref[...] = src_ref[...].astype(jnp.bfloat16).astype(jnp.float32)
    row_ref[pl.ds(0, none_rel), :] = rel_ref[...] * (0.5 * rel_ref.shape[1] ** -0.5)
    row_ref[pl.ds(none_rel, 8), :] = jnp.zeros((8, rel_ref.shape[1]), jnp.float32)
    for k in range(rounds):
        live = counts[k]

        def count(t, c):
            e = key(tiles[k, t])
            return tuple(c[i] + jnp.where(e == i, 1, 0) for i in range(number))

        amount = lax.fori_loop(0, live, count, (jnp.int32(0),) * number)
        starts = [jnp.int32(0)]
        for i in range(number):
            starts.append(starts[-1] + ((amount[i] + GROUP - 1) // GROUP) * GROUP)
        for i in range(number + 1):
            plan[k, i] = starts[i] // GROUP

        def place(t, at):
            code = tiles[k, t]
            e = key(code)
            p = at[0]
            for i in range(1, number):
                p = jnp.where(e == i, at[i], p)
            plan[k, number + 1 + p] = (code // number) * (none_rel + 1) + rel[k, t]
            return tuple(at[i] + jnp.where(e == i, 1, 0) for i in range(number))

        ends = lax.fori_loop(0, live, place, tuple(starts[:-1]))
        for i in range(number):

            def pad(p, carry):
                plan[k, number + 1 + p] = none_rel
                return carry

            lax.fori_loop(ends[i], starts[i + 1], pad, 0)


def prep(tiles, rel, counts, src_table, rel_table, shard_blocks):
    rounds, slots = tiles.shape
    reps = lax.axis_size("rep")
    length = slots + reps * shard_blocks * (GROUP + 1) + 1
    rep = lax.axis_index("rep").astype(jnp.int32).reshape(1)
    return pl.pallas_call(
        functools.partial(prep_kernel, reps, shard_blocks),
        in_specs=[SMEM] * 4 + [VMEM] * 2,
        out_specs=[SMEM, VMEM, VMEM],
        out_shape=[
            jax.ShapeDtypeStruct((rounds, length), jnp.int32),
            jax.ShapeDtypeStruct(src_table.shape, jnp.float32),
            jax.ShapeDtypeStruct((rel_table.shape[0] + 8, rel_table.shape[1]), jnp.float32),
        ],
        compiler_params=GRANT,
        name="prepare",
    )(rep, tiles, rel, counts, src_table, rel_table)


def tile_kernel(round_index, blocks, shard_blocks, number, carried, plan, low_ref, row_ref, *refs):
    shards, refs = refs[: len(blocks)], refs[len(blocks) + carried :]
    src_grad, parts, dst_grad = refs[0], refs[1 : 1 + len(blocks)], refs[1 + len(blocks)]
    rels = row_ref.shape[0] - 7
    if not carried:
        src_grad[...] = jnp.zeros_like(src_grad)
    row_id = lax.broadcasted_iota(jnp.int32, (TILE, TILE), 0)
    column_id = lax.broadcasted_iota(jnp.int32, (TILE, TILE), 1)
    offset = jnp.where(row_id == column_id, -1.0, 1.0).astype(jnp.float32)
    for at, block in enumerate(blocks):
        for i in range(shard_blocks):
            dst = shards[at][pl.ds(i * TILE, TILE), :]
            dst_grad[...] = jnp.zeros_like(dst_grad)

            def step(q, carry):
                where, rows, low = [], [], []
                for g in range(GROUP):
                    code = plan[round_index, number + 1 + q * GROUP + g]
                    s = pl.multiple_of(code // rels * TILE, TILE)
                    row = row_ref[pl.ds(lax.rem(code, rels), 1), :]
                    where.append(s)
                    rows.append(row)
                    low.append((low_ref[pl.ds(s, TILE), :] * row).astype(jnp.bfloat16))
                src_rel = jnp.concatenate(low, 0)
                scores = lax.dot_general(
                    src_rel, dst, (((1,), (1,)), ((), ())), preferred_element_type=jnp.float32
                )
                slope = jnp.concatenate(
                    [
                        (jnp.tanh(scores[g * TILE : (g + 1) * TILE]) + offset).astype(jnp.bfloat16)
                        for g in range(GROUP)
                    ],
                    0,
                )
                src_terms = jnp.dot(slope, dst, preferred_element_type=jnp.float32)
                dst_grad[...] += lax.dot_general(
                    slope, src_rel, (((0,), (0,)), ((), ())), preferred_element_type=jnp.float32
                )
                for g in range(GROUP):
                    src_grad[pl.ds(where[g], TILE), :] += (
                        src_terms[g * TILE : (g + 1) * TILE] * rows[g]
                    )
                return carry

            lax.fori_loop(
                plan[round_index, block * shard_blocks + i],
                plan[round_index, block * shard_blocks + i + 1],
                step,
                0,
            )
            parts[at][pl.ds(i * TILE, TILE), :] = dst_grad[...].astype(jnp.bfloat16)


def tile_work(round_index, blocks, plan, low, rel_rows, shards, src_grad):
    reps = lax.axis_size("rep")
    shard, width = shards[0].shape
    slots = plan.shape[1] * len(blocks) // reps
    carried = [] if src_grad is None else [src_grad]
    out = pl.pallas_call(
        functools.partial(
            tile_kernel, round_index, blocks, shard // TILE, reps * (shard // TILE), len(carried)
        ),
        in_specs=[SMEM] + [VMEM] * (2 + len(blocks) + len(carried)),
        out_specs=[VMEM] * (1 + len(blocks)),
        out_shape=[jax.ShapeDtypeStruct(low.shape, jnp.float32)]
        + [jax.ShapeDtypeStruct((shard, width), jnp.bfloat16)] * len(blocks),
        scratch_shapes=[pltpu.VMEM((TILE, width), jnp.float32)],
        input_output_aliases={3 + len(blocks): 0} if carried else {},
        cost_estimate=pl.CostEstimate(
            flops=6 * slots * TILE * TILE * width,
            bytes_accessed=4 * low.size,
            transcendentals=slots * TILE * TILE,
        ),
        compiler_params=GRANT,
        name="tile_work",
    )(plan, low, rel_rows, *shards, *carried)
    return out[0], list(out[1:])


def adagrad_kernel(sums, table_ref, state_ref, *refs):
    grads, (table_out, state_out, low_out) = refs[:sums], refs[sums:]
    width = table_ref.shape[1]
    row_id = lax.broadcasted_iota(jnp.int32, (TILE, TILE), 0)
    column_id = lax.broadcasted_iota(jnp.int32, (TILE, TILE), 1)
    same = row_id == column_id

    def block(i, carry):
        rows = pl.ds(pl.multiple_of(i * TILE, TILE), TILE)
        grad = grads[0][rows, :].astype(jnp.float32)
        for other in grads[1:]:
            grad = grad + other[rows, :].astype(jnp.float32)
        if sums > 1:
            grad = grad.astype(jnp.bfloat16).astype(jnp.float32)
        state = jnp.sum(jnp.where(same, state_ref[pl.ds(i, 1), :], 0.0), axis=1, keepdims=True)
        state = state + jnp.sum(grad * grad, axis=1, keepdims=True) * (1.0 / width)
        state_out[pl.ds(i, 1), :] = jnp.sum(jnp.where(same, state, 0.0), axis=0, keepdims=True)
        table = table_ref[rows, :] - learn_rate * grad / jnp.sqrt(state)
        table_out[rows, :] = table
        low_out[rows, :] = table.astype(jnp.bfloat16).astype(low_out.dtype)
        return carry

    lax.fori_loop(0, table_ref.shape[0] // TILE, block, 0)


def adagrad(table, state, grads, low_type):
    return pl.pallas_call(
        functools.partial(adagrad_kernel, len(grads)),
        in_specs=[VMEM] * (2 + len(grads)),
        out_specs=[VMEM] * 3,
        out_shape=[
            jax.ShapeDtypeStruct(table.shape, jnp.float32),
            jax.ShapeDtypeStruct(state.shape, jnp.float32),
            jax.ShapeDtypeStruct(table.shape, low_type),
        ],
        cost_estimate=pl.CostEstimate(
            flops=8 * table.size, bytes_accessed=8 * table.size, transcendentals=table.shape[0]
        ),
        compiler_params=GRANT,
        name="adagrad",
    )(table, state, *grads)


def per_device(
    src_table, src_state, dst_table, dst_state, rel_table, partners, tiles, tile_rel, counts
):
    reps = lax.axis_size("rep")
    rounds = partners.shape[0]
    shard_blocks = dst_table.shape[0] // TILE
    src_state = src_state.reshape(-1, TILE)
    dst_state = dst_state.reshape(-1, TILE)
    low_chunk, *high_chunks = bit_chunks()
    pieces = [tuple(range(reps))[i :: PIECES] for i in range(min(PIECES, reps))]
    rows = dst_table.astype(jnp.bfloat16)
    plan = low = rel_rows = None

    for k in range(rounds):

        def branch(value, operands, k=k):
            rows, src_table, src_state, extra = operands
            arrived = [send(rows, value, j) for j in range(reps)]
            if k == 0:
                extra = prep(*extra, src_table, rel_table, shard_blocks)
            plan, low, rel_rows = extra
            src_grad, returned = None, [None] * reps
            for blocks in pieces:
                src_grad, parts = tile_work(
                    k, blocks, plan, low, rel_rows, [arrived[j] for j in blocks], src_grad
                )
                for j, part in zip(blocks, parts):
                    returned[j] = send(part, value, j)
            src_table, src_state, low = adagrad(src_table, src_state, [src_grad], jnp.float32)
            return returned, src_table, src_state, (plan, low, rel_rows)

        extra = (tiles[0, 0], tile_rel[0, 0], counts[0, 0]) if k == 0 else (plan, low, rel_rows)
        mask = partners[k, 0]
        returned, src_table, src_state, (plan, low, rel_rows) = by_mask(
            mask, low_chunk, branch, (send_high(rows, mask), src_table, src_state, extra)
        )
        if high_chunks:
            total = functools.reduce(jnp.add, [x.astype(jnp.float32) for x in returned])
            returned = [send_high(total.astype(jnp.bfloat16), mask)]
        dst_table, dst_state, rows = adagrad(dst_table, dst_state, returned, jnp.bfloat16)
    return (src_table, src_state.reshape(-1), dst_table, dst_state.reshape(-1))


def solution(mesh):
    table, state = P(AXES, None), P(AXES)
    in_specs = (
        table,
        state,
        table,
        state,
        P(),
        P(),
        P("bucket", "rep", None, None),
        P("bucket", "rep", None, None),
        P("bucket", "rep", None),
    )
    return jax.shard_map(
        per_device,
        mesh=mesh,
        in_specs=in_specs,
        out_specs=(table, state, table, state),
        check_vma=False,
    )
```

```python
import functools

import jax
import jax.numpy as jnp
from jax import lax
from jax.experimental import pallas as pl
from jax.experimental.pallas import tpu as pltpu
from jax.sharding import PartitionSpec as P

TILE = 128
GROUP = 4
LOW_BITS = 3
SHIFT = 16

learn_rate = 0.1

AXES = ("bucket", "rep")
SMEM = pl.BlockSpec(memory_space=pltpu.SMEM)
VMEM = pl.BlockSpec(memory_space=pltpu.VMEM)
GRANT = pltpu.CompilerParams(vmem_limit_bytes=12 * 1024 * 1024)


def bucket_send(rows, mask):
    buckets = lax.axis_size("bucket")
    bits = buckets.bit_length() - 1
    for first in range(0, bits, LOW_BITS):
        width = min(LOW_BITS, bits - first)
        least = 1 if width == bits else 0

        def branch(value, x, first=first):
            if value == 0:
                return x
            return lax.ppermute(x, "bucket", [(b, b ^ (value << first)) for b in range(buckets)])

        index = jnp.bitwise_and(jnp.right_shift(mask, first), (1 << width) - 1) - least
        branches = [functools.partial(branch, value) for value in range(least, 1 << width)]
        rows = lax.switch(index, branches, rows)
    return rows


def rep_send(rows, offset):
    if offset == 0:
        return rows
    return lax.ppermute(rows, "rep", [(r, r ^ offset) for r in range(lax.axis_size("rep"))])


def prep_kernel(reps, shard_blocks, room, rep, tiles, rel, counts, src_ref, rel_ref, plan, low_ref, row_ref):
    rounds, slots = tiles.shape
    number = reps * shard_blocks
    bits = number.bit_length() - 1
    none_rel = rel_ref.shape[0]
    flip = rep[0] * shard_blocks
    low_ref[...] = src_ref[...].astype(jnp.bfloat16).astype(jnp.float32)
    row_ref[pl.ds(0, none_rel), :] = rel_ref[...] * (0.5 * rel_ref.shape[1] ** -0.5)
    row_ref[pl.ds(none_rel, 8), :] = jnp.zeros((8, rel_ref.shape[1]), jnp.float32)
    for k in range(rounds):

        def place(t, ends, k=k):
            code = tiles[k, t]
            e = jnp.bitwise_xor(jnp.bitwise_and(code, number - 1), flip)
            p = ends[0]
            for i in range(1, number):
                p = jnp.where(e == i, ends[i], p)
            plan[k, number + e * room + p] = jnp.bitwise_or(
                jnp.left_shift(jnp.right_shift(code, bits), SHIFT), rel[k, t]
            )
            return tuple(ends[i] + jnp.where(e == i, 1, 0) for i in range(number))

        ends = lax.fori_loop(0, counts[k], place, (jnp.int32(0),) * number)
        for i in range(number):
            plan[k, i] = jnp.right_shift(ends[i] + (GROUP - 1), GROUP.bit_length() - 1)
            for extra in range(2 * GROUP):
                plan[k, number + i * room + ends[i] + extra] = jnp.int32(none_rel)


def prep(tiles, rel, counts, src_table, rel_table, shard_blocks):
    rounds, slots = tiles.shape
    reps = lax.axis_size("rep")
    number = reps * shard_blocks
    room = slots + 2 * GROUP
    rep = lax.axis_index("rep").astype(jnp.int32).reshape(1)
    return pl.pallas_call(
        functools.partial(prep_kernel, reps, shard_blocks, room),
        in_specs=[SMEM] * 4 + [VMEM] * 2,
        out_specs=[SMEM, VMEM, VMEM],
        out_shape=[
            jax.ShapeDtypeStruct((rounds, number * (room + 1)), jnp.int32),
            jax.ShapeDtypeStruct(src_table.shape, jnp.float32),
            jax.ShapeDtypeStruct((rel_table.shape[0] + 8, rel_table.shape[1]), jnp.float32),
        ],
        cost_estimate=pl.CostEstimate(flops=0, bytes_accessed=3 * 1024 * 1024, transcendentals=0),
        compiler_params=GRANT,
        name="prepare",
    )(rep, tiles, rel, counts, src_table, rel_table)


def tile_kernel(round_index, block, number, room, carried, plan, low_ref, row_ref, dst_ref, *refs):
    src_grad, part, dst_grad, held_rows, held_slope = refs[carried:]
    shard_blocks = dst_ref.shape[0] // TILE
    if not carried:
        src_grad[...] = jnp.zeros_like(src_grad)
    row_id = lax.broadcasted_iota(jnp.int32, (TILE, TILE), 0)
    column_id = lax.broadcasted_iota(jnp.int32, (TILE, TILE), 1)
    offset = jnp.where(row_id == column_id, -1.0, 1.0).astype(jnp.float32)
    for i in range(shard_blocks):
        at = block * shard_blocks + i
        dst_rows = pl.ds(i * TILE, TILE)
        steps = plan[round_index, at]
        dst_grad[...] = jnp.zeros_like(dst_grad)

        def group(q, at=at):
            where, rows = [], []
            for g in range(GROUP):
                code = plan[round_index, number + at * room + q * GROUP + g]
                where.append(pl.multiple_of(jnp.right_shift(code, SHIFT) * TILE, TILE))
                rows.append(row_ref[pl.ds(jnp.bitwise_and(code, (1 << SHIFT) - 1), 1), :])
            return where, rows

        def slopes(q, slot, dst_rows=dst_rows):
            where, rows = group(q)
            src_rel = jnp.concatenate(
                [(low_ref[pl.ds(s, TILE), :] * row).astype(jnp.bfloat16) for s, row in zip(where, rows)],
                0,
            )
            scores = lax.dot_general(
                src_rel, dst_ref[dst_rows, :], (((1,), (1,)), ((), ())),
                preferred_element_type=jnp.float32,
            )
            slope = jnp.concatenate(
                [
                    (jnp.tanh(scores[g * TILE : (g + 1) * TILE]) + offset).astype(jnp.bfloat16)
                    for g in range(GROUP)
                ],
                0,
            )
            held_rows[slot] = src_rel
            held_slope[slot] = slope

        def grads(q, slot, dst_rows=dst_rows):
            where, rows = group(q)
            slope = held_slope[slot]
            src_terms = jnp.dot(slope, dst_ref[dst_rows, :], preferred_element_type=jnp.float32)
            dst_grad[...] += lax.dot_general(
                slope, held_rows[slot], (((0,), (0,)), ((), ())), preferred_element_type=jnp.float32
            )
            for g in range(GROUP):
                src_grad[pl.ds(where[g], TILE), :] += src_terms[g * TILE : (g + 1) * TILE] * rows[g]

        @pl.when(steps > 0)
        def _():
            slopes(0, 0)

            def two(p, carry):
                q = p * 2
                slopes(q + 1, 1)
                grads(q, 0)
                slopes(q + 2, 0)
                grads(q + 1, 1)
                return carry

            lax.fori_loop(0, jnp.right_shift(steps, 1), two, 0)

            @pl.when(jnp.bitwise_and(steps, 1) == 1)
            def _():
                grads(steps - 1, 0)

        part[dst_rows, :] = dst_grad[...].astype(jnp.bfloat16)


def tile_work(round_index, block, plan, low, rel_rows, shard, src_grad):
    reps = lax.axis_size("rep")
    rows, width = shard.shape
    number = reps * (rows // TILE)
    room = plan.shape[1] // number - 1
    slots = room // reps
    carried = [] if src_grad is None else [src_grad]
    return pl.pallas_call(
        functools.partial(tile_kernel, round_index, block, number, room, len(carried)),
        in_specs=[SMEM] + [VMEM] * (3 + len(carried)),
        out_specs=[VMEM] * 2,
        out_shape=[
            jax.ShapeDtypeStruct(low.shape, jnp.float32),
            jax.ShapeDtypeStruct((rows, width), jnp.bfloat16),
        ],
        scratch_shapes=[
            pltpu.VMEM((TILE, width), jnp.float32),
            pltpu.VMEM((2, GROUP * TILE, width), jnp.bfloat16),
            pltpu.VMEM((2, GROUP * TILE, TILE), jnp.bfloat16),
        ],
        input_output_aliases={4: 0} if carried else {},
        cost_estimate=pl.CostEstimate(
            flops=6 * slots * TILE * TILE * width,
            bytes_accessed=4 * low.size,
            transcendentals=slots * TILE * TILE,
        ),
        compiler_params=GRANT,
        name="tile_work",
    )(plan, low, rel_rows, shard, *carried)


def adagrad_kernel(table_ref, state_ref, grad_ref, table_out, state_out, low_out):
    width = table_ref.shape[1]
    row_id = lax.broadcasted_iota(jnp.int32, (TILE, TILE), 0)
    column_id = lax.broadcasted_iota(jnp.int32, (TILE, TILE), 1)
    same = row_id == column_id

    def block(i, carry):
        rows = pl.ds(pl.multiple_of(i * TILE, TILE), TILE)
        grad = grad_ref[rows, :].astype(jnp.float32)
        state = jnp.sum(jnp.where(same, state_ref[pl.ds(i, 1), :], 0.0), axis=1, keepdims=True)
        state = state + jnp.sum(grad * grad, axis=1, keepdims=True) * (1.0 / width)
        state_out[pl.ds(i, 1), :] = jnp.sum(jnp.where(same, state, 0.0), axis=0, keepdims=True)
        table = table_ref[rows, :] - learn_rate * grad / jnp.sqrt(state)
        table_out[rows, :] = table
        low_out[rows, :] = table.astype(jnp.bfloat16).astype(low_out.dtype)
        return carry

    lax.fori_loop(0, table_ref.shape[0] // TILE, block, 0)


def adagrad(table, state, grad, low_type):
    return pl.pallas_call(
        adagrad_kernel,
        in_specs=[VMEM] * 3,
        out_specs=[VMEM] * 3,
        out_shape=[
            jax.ShapeDtypeStruct(table.shape, jnp.float32),
            jax.ShapeDtypeStruct(state.shape, jnp.float32),
            jax.ShapeDtypeStruct(table.shape, low_type),
        ],
        cost_estimate=pl.CostEstimate(
            flops=8 * table.size, bytes_accessed=8 * table.size, transcendentals=table.shape[0]
        ),
        compiler_params=GRANT,
        name="adagrad",
    )(table, state, grad)


def per_device(
    src_table, src_state, dst_table, dst_state, rel_table, partners, tiles, tile_rel, counts
):
    reps = lax.axis_size("rep")
    rounds = partners.shape[0]
    src_state = src_state.reshape(-1, TILE)
    dst_state = dst_state.reshape(-1, TILE)
    plan, low, rel_rows = prep(
        tiles[0, 0], tile_rel[0, 0], counts[0, 0], src_table, rel_table, dst_table.shape[0] // TILE
    )
    rows = dst_table.astype(jnp.bfloat16)
    for k in range(rounds):
        mask = partners[k, 0]
        own = bucket_send(rows, mask)
        shards = [rep_send(own, j) for j in range(reps)]
        src_grad, total = None, None
        for j in range(reps):
            src_grad, part = tile_work(k, j, plan, low, rel_rows, shards[j], src_grad)
            part = rep_send(part, j).astype(jnp.float32)
            total = part if total is None else total + part
        total = bucket_send(total.astype(jnp.bfloat16), mask)
        src_table, src_state, low = adagrad(src_table, src_state, src_grad, jnp.float32)
        dst_table, dst_state, rows = adagrad(dst_table, dst_state, total, jnp.bfloat16)
    return (src_table, src_state.reshape(-1), dst_table, dst_state.reshape(-1))


def solution(mesh):
    table, state = P(AXES, None), P(AXES)
    in_specs = (
        table,
        state,
        table,
        state,
        P(),
        P(),
        P("bucket", "rep", None, None),
        P("bucket", "rep", None, None),
        P("bucket", "rep", None),
    )
    return jax.shard_map(
        per_device,
        mesh=mesh,
        in_specs=in_specs,
        out_specs=(table, state, table, state),
        check_vma=False,
    )
```

```python
import functools

import jax
import jax.numpy as jnp
from jax import lax
from jax.experimental import pallas as pl
from jax.experimental.pallas import tpu as pltpu
from jax.sharding import PartitionSpec as P

TILE = 128
GROUP = 4
LOW_BITS = 3
SHIFT = 16

learn_rate = 0.1

AXES = ("bucket", "rep")
SMEM = pl.BlockSpec(memory_space=pltpu.SMEM)
VMEM = pl.BlockSpec(memory_space=pltpu.VMEM)
GRANT = pltpu.CompilerParams(vmem_limit_bytes=12 * 1024 * 1024)


def bucket_send(rows, mask):
    buckets = lax.axis_size("bucket")
    bits = buckets.bit_length() - 1
    for first in range(0, bits, LOW_BITS):
        width = min(LOW_BITS, bits - first)
        least = 1 if width == bits else 0

        def branch(value, x, first=first):
            if value == 0:
                return x
            return lax.ppermute(x, "bucket", [(b, b ^ (value << first)) for b in range(buckets)])

        if width == bits:
            index = mask - 1
        else:
            index = jnp.bitwise_and(jnp.right_shift(mask, first), (1 << width) - 1)
        branches = [functools.partial(branch, value) for value in range(least, 1 << width)]
        rows = lax.switch(index, branches, rows)
    return rows


def rep_send(rows, offset):
    if offset == 0:
        return rows
    return lax.ppermute(rows, "rep", [(r, r ^ offset) for r in range(lax.axis_size("rep"))])


def sort_tiles(k, number, room, flip, none_rel, tiles, rel, counts, plan):
    bits = number.bit_length() - 1

    def place(t, ends):
        code = tiles[k, t]
        e = jnp.bitwise_xor(jnp.bitwise_and(code, number - 1), flip)
        p = ends[0]
        for i in range(1, number):
            p = jnp.where(e == i, ends[i], p)
        plan[0, number + e * room + p] = jnp.bitwise_or(
            jnp.left_shift(jnp.right_shift(code, bits), SHIFT), rel[k, t]
        )
        return tuple(ends[i] + jnp.where(e == i, 1, 0) for i in range(number))

    ends = lax.fori_loop(0, counts[k], place, (jnp.int32(0),) * number)
    for i in range(number):
        plan[0, i] = jnp.right_shift(ends[i] + (GROUP - 1), GROUP.bit_length() - 1)
        for extra in range(2 * GROUP):
            plan[0, number + i * room + ends[i] + extra] = jnp.int32(none_rel)


def first_kernel(rounds, number, room, none_rel, rep, tiles, rel, counts, partners, dst_ref, plan, rows_ref, *masks):
    shard_blocks = dst_ref.shape[0] // TILE
    rows_ref[...] = dst_ref[...].astype(jnp.bfloat16)
    for k in range(rounds):
        masks[k][0, 0] = partners[k, 0]
    sort_tiles(0, number, room, rep[0] * shard_blocks, none_rel, tiles, rel, counts, plan)


def later_kernel(k, shard_blocks, number, room, none_rel, rep, tiles, rel, counts, plan):
    sort_tiles(k, number, room, rep[0] * shard_blocks, none_rel, tiles, rel, counts, plan)


def round_kernel(src_ref, rel_ref, low_ref, row_ref):
    rels, width = rel_ref.shape
    low_ref[...] = src_ref[...].astype(jnp.bfloat16).astype(jnp.float32)
    row_ref[pl.ds(0, rels), :] = rel_ref[...] * (0.5 * width**-0.5)
    row_ref[pl.ds(rels, 8), :] = jnp.zeros((8, width), jnp.float32)


def round_source(src_table, rel_table):
    return pl.pallas_call(
        round_kernel,
        in_specs=[VMEM] * 2,
        out_specs=[VMEM] * 2,
        out_shape=[
            jax.ShapeDtypeStruct(src_table.shape, jnp.float32),
            jax.ShapeDtypeStruct((rel_table.shape[0] + 8, rel_table.shape[1]), jnp.float32),
        ],
        cost_estimate=pl.CostEstimate(
            flops=src_table.size, bytes_accessed=8 * src_table.size, transcendentals=0
        ),
        compiler_params=GRANT,
        name="round_source",
    )(src_table, rel_table)


def tile_kernel(block, number, room, carried, plan, low_ref, row_ref, dst_ref, *refs):
    src_grad, part, dst_grad, held_rows, held_slope = refs[carried:]
    shard_blocks = dst_ref.shape[0] // TILE
    if not carried:
        src_grad[...] = jnp.zeros_like(src_grad)
    row_id = lax.broadcasted_iota(jnp.int32, (TILE, TILE), 0)
    column_id = lax.broadcasted_iota(jnp.int32, (TILE, TILE), 1)
    offset = jnp.where(row_id == column_id, -1.0, 1.0).astype(jnp.float32)
    for i in range(shard_blocks):
        at = block * shard_blocks + i
        dst_rows = pl.ds(i * TILE, TILE)
        steps = plan[0, at]
        dst_grad[...] = jnp.zeros_like(dst_grad)

        def group(q, at=at):
            where, rows = [], []
            for g in range(GROUP):
                code = plan[0, number + at * room + q * GROUP + g]
                where.append(pl.multiple_of(jnp.right_shift(code, SHIFT) * TILE, TILE))
                rows.append(row_ref[pl.ds(jnp.bitwise_and(code, (1 << SHIFT) - 1), 1), :])
            return where, rows

        def slopes(q, slot, dst_rows=dst_rows):
            where, rows = group(q)
            src_rel = jnp.concatenate(
                [(low_ref[pl.ds(s, TILE), :] * row).astype(jnp.bfloat16) for s, row in zip(where, rows)],
                0,
            )
            scores = lax.dot_general(
                src_rel, dst_ref[dst_rows, :], (((1,), (1,)), ((), ())),
                preferred_element_type=jnp.float32,
            )
            slope = jnp.concatenate(
                [
                    (jnp.tanh(scores[g * TILE : (g + 1) * TILE]) + offset).astype(jnp.bfloat16)
                    for g in range(GROUP)
                ],
                0,
            )
            held_rows[slot] = src_rel
            held_slope[slot] = slope

        def grads(q, slot, dst_rows=dst_rows):
            where, rows = group(q)
            slope = held_slope[slot]
            src_terms = jnp.dot(slope, dst_ref[dst_rows, :], preferred_element_type=jnp.float32)
            dst_grad[...] += lax.dot_general(
                slope, held_rows[slot], (((0,), (0,)), ((), ())), preferred_element_type=jnp.float32
            )
            for g in range(GROUP):
                src_grad[pl.ds(where[g], TILE), :] += src_terms[g * TILE : (g + 1) * TILE] * rows[g]

        @pl.when(steps > 0)
        def _():
            slopes(0, 0)

            def two(p, carry):
                q = p * 2
                slopes(q + 1, 1)
                grads(q, 0)
                slopes(q + 2, 0)
                grads(q + 1, 1)
                return carry

            lax.fori_loop(0, jnp.right_shift(steps, 1), two, 0)

            @pl.when(jnp.bitwise_and(steps, 1) == 1)
            def _():
                grads(steps - 1, 0)

        part[dst_rows, :] = dst_grad[...].astype(jnp.bfloat16)


def tile_work(block, plan, low, rel_rows, shard, src_grad):
    reps = lax.axis_size("rep")
    rows, width = shard.shape
    number = reps * (rows // TILE)
    room = plan.shape[1] // number - 1
    slots = room // reps
    carried = [] if src_grad is None else [src_grad]
    return pl.pallas_call(
        functools.partial(tile_kernel, block, number, room, len(carried)),
        in_specs=[SMEM] + [VMEM] * (3 + len(carried)),
        out_specs=[VMEM] * 2,
        out_shape=[
            jax.ShapeDtypeStruct(low.shape, jnp.float32),
            jax.ShapeDtypeStruct((rows, width), jnp.bfloat16),
        ],
        scratch_shapes=[
            pltpu.VMEM((TILE, width), jnp.float32),
            pltpu.VMEM((2, GROUP * TILE, width), jnp.bfloat16),
            pltpu.VMEM((2, GROUP * TILE, TILE), jnp.bfloat16),
        ],
        input_output_aliases={4: 0} if carried else {},
        cost_estimate=pl.CostEstimate(
            flops=6 * slots * TILE * TILE * width,
            bytes_accessed=4 * low.size,
            transcendentals=slots * TILE * TILE,
        ),
        compiler_params=GRANT,
        name="tile_work",
    )(plan, low, rel_rows, shard, *carried)


def adagrad_kernel(table_ref, state_ref, grad_ref, table_out, state_out, low_out):
    width = table_ref.shape[1]
    row_id = lax.broadcasted_iota(jnp.int32, (TILE, TILE), 0)
    column_id = lax.broadcasted_iota(jnp.int32, (TILE, TILE), 1)
    same = row_id == column_id

    def block(i, carry):
        rows = pl.ds(pl.multiple_of(i * TILE, TILE), TILE)
        grad = grad_ref[rows, :].astype(jnp.float32)
        state = jnp.sum(jnp.where(same, state_ref[pl.ds(i, 1), :], 0.0), axis=1, keepdims=True)
        state = state + jnp.sum(grad * grad, axis=1, keepdims=True) * (1.0 / width)
        state_out[pl.ds(i, 1), :] = jnp.sum(jnp.where(same, state, 0.0), axis=0, keepdims=True)
        table = table_ref[rows, :] - learn_rate * grad / jnp.sqrt(state)
        table_out[rows, :] = table
        low_out[rows, :] = table.astype(jnp.bfloat16).astype(low_out.dtype)
        return carry

    lax.fori_loop(0, table_ref.shape[0] // TILE, block, 0)


def adagrad(table, state, grad, low_type):
    return pl.pallas_call(
        adagrad_kernel,
        in_specs=[VMEM] * 3,
        out_specs=[VMEM] * 3,
        out_shape=[
            jax.ShapeDtypeStruct(table.shape, jnp.float32),
            jax.ShapeDtypeStruct(state.shape, jnp.float32),
            jax.ShapeDtypeStruct(table.shape, low_type),
        ],
        cost_estimate=pl.CostEstimate(
            flops=8 * table.size, bytes_accessed=8 * table.size, transcendentals=table.shape[0]
        ),
        compiler_params=GRANT,
        name="adagrad",
    )(table, state, grad)


def per_device(
    src_table, src_state, dst_table, dst_state, rel_table, partners, tiles, tile_rel, counts
):
    reps = lax.axis_size("rep")
    rounds = partners.shape[0]
    src_state = src_state.reshape(-1, TILE)
    dst_state = dst_state.reshape(-1, TILE)
    shard_blocks = dst_table.shape[0] // TILE
    number = reps * shard_blocks
    room = tiles.shape[-1] + 2 * GROUP
    none_rel = rel_table.shape[0]
    scalars = (
        lax.axis_index("rep").astype(jnp.int32).reshape(1), tiles[0, 0], tile_rel[0, 0], counts[0, 0],
    )
    plan_shape = jax.ShapeDtypeStruct((1, number * (room + 1)), jnp.int32)
    plan, rows, *masks = pl.pallas_call(
        functools.partial(first_kernel, rounds, number, room, none_rel),
        in_specs=[SMEM] * 5 + [VMEM],
        out_specs=[SMEM, VMEM] + [SMEM] * rounds,
        out_shape=[plan_shape, jax.ShapeDtypeStruct(dst_table.shape, jnp.bfloat16)]
        + [jax.ShapeDtypeStruct((1, 1), jnp.int32)] * rounds,
        compiler_params=GRANT,
        name="first",
    )(*scalars, partners, dst_table)
    for k in range(rounds):
        mask = masks[k].reshape(())
        own = bucket_send(rows, mask)
        shards = [own]
        for j in range(1, reps):
            shards.append(rep_send(own, j))
        if k == 0:
            low, rel_rows = round_source(src_table, rel_table)
        src_grad, total = None, None
        for j in [*range(1, reps), 0]:
            src_grad, part = tile_work(j, plan, low, rel_rows, shards[j], src_grad)
            part = rep_send(part, j)
            part = part.astype(jnp.float32)
            total = part if total is None else total + part
        src_table, src_state, low = adagrad(src_table, src_state, src_grad, jnp.float32)
        if k + 1 < rounds:
            plan = pl.pallas_call(
                functools.partial(later_kernel, k + 1, shard_blocks, number, room, none_rel),
                in_specs=[SMEM] * 4,
                out_specs=SMEM,
                out_shape=plan_shape,
                compiler_params=GRANT,
                name="later",
            )(*scalars)
        total = bucket_send(total.astype(jnp.bfloat16), mask)
        dst_table, dst_state, rows = adagrad(dst_table, dst_state, total, jnp.bfloat16)
    return (src_table, src_state.reshape(-1), dst_table, dst_state.reshape(-1))


def solution(mesh):
    table, state = P(AXES, None), P(AXES)
    in_specs = (
        table,
        state,
        table,
        state,
        P(),
        P(),
        P("bucket", "rep", None, None),
        P("bucket", "rep", None, None),
        P("bucket", "rep", None),
    )
    return jax.shard_map(
        per_device,
        mesh=mesh,
        in_specs=in_specs,
        out_specs=(table, state, table, state),
        check_vma=False,
    )
```

```python
import functools

import jax
import jax.numpy as jnp
from jax import lax
from jax.experimental import pallas as pl
from jax.experimental.pallas import tpu as pltpu
from jax.sharding import PartitionSpec as P

TILE = 128
GROUP = 4
LOW_BITS = 3
SHIFT = 16

learn_rate = 0.1

AXES = ("bucket", "rep")
SMEM = pl.BlockSpec(memory_space=pltpu.SMEM)
VMEM = pl.BlockSpec(memory_space=pltpu.VMEM)
FIRST_GRANT = 60 * 1024 * 1024
GRANT = pltpu.CompilerParams(vmem_limit_bytes=12 * 1024 * 1024)


def bucket_send(rows, mask):
    buckets = lax.axis_size("bucket")
    bits = buckets.bit_length() - 1
    for first in range(0, bits, LOW_BITS):
        width = min(LOW_BITS, bits - first)
        least = 1 if width == bits else 0

        def branch(value, x, first=first):
            if value == 0:
                return x
            return lax.ppermute(x, "bucket", [(b, b ^ (value << first)) for b in range(buckets)])

        if width == bits:
            index = mask - 1
        else:
            index = jnp.bitwise_and(jnp.right_shift(mask, first), (1 << width) - 1)
        branches = [functools.partial(branch, value) for value in range(least, 1 << width)]
        rows = lax.switch(index, branches, rows)
    return rows


def rep_send(rows, offset):
    if offset == 0:
        return rows
    return lax.ppermute(rows, "rep", [(r, r ^ offset) for r in range(lax.axis_size("rep"))])


def layout(number, slots):
    most = slots // GROUP + number + 3
    first = 2
    second = first + most
    start = second + most
    room = 1 << (slots + 2 * GROUP - 1).bit_length()
    return first, second, start, room, start + number * room


def sort_tiles(k, own, none_rel, flip, number, tiles, rel, counts, plan):
    bits = number.bit_length() - 1
    first, second, start, room, _ = layout(number, tiles.shape[1])

    def place(t, ends):
        code = tiles[k, t]
        e = jnp.bitwise_xor(jnp.bitwise_and(code, number - 1), flip)
        p = ends[0]
        for i in range(1, number):
            p = jnp.where(e == i, ends[i], p)
        plan[0, start + e * room + p] = jnp.bitwise_or(
            jnp.left_shift(jnp.right_shift(code, bits), SHIFT), rel[k, t]
        )
        return tuple(ends[i] + jnp.where(e == i, 1, 0) for i in range(number))

    ends = lax.fori_loop(0, counts[k], place, (jnp.int32(0),) * number)
    for i in range(number):
        for extra in range(2 * GROUP):
            plan[0, start + i * room + ends[i] + extra] = jnp.int32(none_rel)
    for index, at, blocks in ((0, first, range(own, number)), (1, second, range(own))):
        q = jnp.int32(0)
        for i in blocks:
            amount = jnp.right_shift(ends[i] + (GROUP - 1), GROUP.bit_length() - 1)

            def name(g, carry, i=i, q=q, at=at):
                plan[0, at + q + g] = i * room + g * GROUP
                return carry

            lax.fori_loop(0, amount, name, 0)
            q = q + amount
        plan[0, index] = q
        for extra in range(3):
            plan[0, at + q + extra] = blocks[0] * room


def first_kernel(rounds, number, none_rel, rep, tiles, rel, counts, partners, dst_ref, plan, rows_ref, *masks):
    own = dst_ref.shape[0] // TILE
    rows_ref[...] = dst_ref[...].astype(jnp.bfloat16)
    for k in range(rounds):
        masks[k][0, 0] = partners[k, 0]
    sort_tiles(0, own, none_rel, rep[0] * own, number, tiles, rel, counts, plan)


def later_kernel(k, own, number, none_rel, rep, tiles, rel, counts, after, plan):
    sort_tiles(k, own, none_rel, rep[0] * own, number, tiles, rel, counts, plan)


def round_kernel(src_ref, rel_ref, low_ref, row_ref):
    rels, width = rel_ref.shape
    low_ref[...] = src_ref[...].astype(jnp.bfloat16).astype(jnp.float32)
    row_ref[pl.ds(0, rels), :] = rel_ref[...] * (0.5 * width**-0.5)
    row_ref[pl.ds(rels, 8), :] = jnp.zeros((8, width), jnp.float32)


def round_source(src_table, rel_table):
    return pl.pallas_call(
        round_kernel,
        in_specs=[VMEM] * 2,
        out_specs=[VMEM] * 2,
        out_shape=[
            jax.ShapeDtypeStruct(src_table.shape, jnp.float32),
            jax.ShapeDtypeStruct((rel_table.shape[0] + 8, rel_table.shape[1]), jnp.float32),
        ],
        cost_estimate=pl.CostEstimate(
            flops=src_table.size, bytes_accessed=8 * src_table.size, transcendentals=0
        ),
        compiler_params=GRANT,
        name="round_source",
    )(src_table, rel_table)


def tile_kernel(index, lists, shards, carried, plan, low_ref, row_ref, *refs):
    dst_refs, refs = refs[:shards], refs[shards + carried :]
    src_grad, parts, refs = refs[0], refs[1 : 1 + shards], refs[1 + shards :]
    dst_all, dst_grad, held_rows, held_slope = refs
    _, _, start, room, _ = lists
    at_list = lists[index]
    rows_of_shard = dst_refs[0].shape[0]
    first_row = rows_of_shard if index == 0 else 0
    if not carried:
        src_grad[...] = jnp.zeros_like(src_grad)
    for i in range(shards):
        dst_all[pl.ds(i * rows_of_shard, rows_of_shard), :] = dst_refs[i][...]
    dst_grad[...] = jnp.zeros_like(dst_grad)
    row_id = lax.broadcasted_iota(jnp.int32, (TILE, TILE), 0)
    column_id = lax.broadcasted_iota(jnp.int32, (TILE, TILE), 1)
    offset = jnp.where(row_id == column_id, -1.0, 1.0).astype(jnp.float32)
    steps = plan[0, index]

    def group(q):
        at = plan[0, at_list + q]
        block = jnp.right_shift(at, room.bit_length() - 1)
        where, rows = [], []
        for g in range(GROUP):
            code = plan[0, start + at + g]
            where.append(pl.multiple_of(jnp.right_shift(code, SHIFT) * TILE, TILE))
            rows.append(row_ref[pl.ds(jnp.bitwise_and(code, (1 << SHIFT) - 1), 1), :])
        return pl.ds(pl.multiple_of(block * TILE - first_row, TILE), TILE), where, rows

    def slopes(q, slot):
        dst_rows, where, rows = group(q)
        src_rel = jnp.concatenate(
            [(low_ref[pl.ds(s, TILE), :] * row).astype(jnp.bfloat16) for s, row in zip(where, rows)], 0
        )
        scores = lax.dot_general(
            src_rel, dst_all[dst_rows, :], (((1,), (1,)), ((), ())), preferred_element_type=jnp.float32
        )
        slope = jnp.concatenate(
            [
                (jnp.tanh(scores[g * TILE : (g + 1) * TILE]) + offset).astype(jnp.bfloat16)
                for g in range(GROUP)
            ],
            0,
        )
        held_rows[slot] = src_rel
        held_slope[slot] = slope

    def grads(q, slot):
        dst_rows, where, rows = group(q)
        slope = held_slope[slot]
        src_terms = jnp.dot(slope, dst_all[dst_rows, :], preferred_element_type=jnp.float32)
        dst_grad[dst_rows, :] += lax.dot_general(
            slope, held_rows[slot], (((0,), (0,)), ((), ())), preferred_element_type=jnp.float32
        )
        for g in range(GROUP):
            src_grad[pl.ds(where[g], TILE), :] += src_terms[g * TILE : (g + 1) * TILE] * rows[g]

    @pl.when(steps > 0)
    def _():
        slopes(0, 0)

        def two(p, carry):
            q = p * 2
            slopes(q + 1, 1)
            grads(q, 0)
            slopes(q + 2, 0)
            grads(q + 1, 1)
            return carry

        lax.fori_loop(0, jnp.right_shift(steps, 1), two, 0)

        @pl.when(jnp.bitwise_and(steps, 1) == 1)
        def _():
            grads(steps - 1, 0)

    for i in range(shards):
        parts[i][...] = dst_grad[pl.ds(i * rows_of_shard, rows_of_shard), :].astype(jnp.bfloat16)


def tile_work(index, lists, slots, plan, low, rel_rows, shards, src_grad):
    rows, width = shards[0].shape
    carried = [] if src_grad is None else [src_grad]
    out = pl.pallas_call(
        functools.partial(tile_kernel, index, lists, len(shards), len(carried)),
        in_specs=[SMEM] + [VMEM] * (2 + len(shards) + len(carried)),
        out_specs=[VMEM] * (1 + len(shards)),
        out_shape=[jax.ShapeDtypeStruct(low.shape, jnp.float32)]
        + [jax.ShapeDtypeStruct((rows, width), jnp.bfloat16)] * len(shards),
        scratch_shapes=[
            pltpu.VMEM((len(shards) * rows, width), jnp.bfloat16),
            pltpu.VMEM((len(shards) * rows, width), jnp.float32),
            pltpu.VMEM((2, GROUP * TILE, width), jnp.bfloat16),
            pltpu.VMEM((2, GROUP * TILE, TILE), jnp.bfloat16),
        ],
        input_output_aliases={3 + len(shards): 0} if carried else {},
        cost_estimate=pl.CostEstimate(
            flops=6 * slots * TILE * TILE * width,
            bytes_accessed=4 * low.size,
            transcendentals=slots * TILE * TILE,
        ),
        compiler_params=GRANT,
        name="tile_work",
    )(plan, low, rel_rows, *shards, *carried)
    return out[0], list(out[1:])


def adagrad_kernel(table_ref, state_ref, grad_ref, table_out, state_out, low_out):
    width = table_ref.shape[1]
    row_id = lax.broadcasted_iota(jnp.int32, (TILE, TILE), 0)
    column_id = lax.broadcasted_iota(jnp.int32, (TILE, TILE), 1)
    same = row_id == column_id

    def block(i, carry):
        rows = pl.ds(pl.multiple_of(i * TILE, TILE), TILE)
        grad = grad_ref[rows, :].astype(jnp.float32)
        state = jnp.sum(jnp.where(same, state_ref[pl.ds(i, 1), :], 0.0), axis=1, keepdims=True)
        state = state + jnp.sum(grad * grad, axis=1, keepdims=True) * (1.0 / width)
        state_out[pl.ds(i, 1), :] = jnp.sum(jnp.where(same, state, 0.0), axis=0, keepdims=True)
        table = table_ref[rows, :] - learn_rate * grad / jnp.sqrt(state)
        table_out[rows, :] = table
        low_out[rows, :] = table.astype(jnp.bfloat16).astype(low_out.dtype)
        return carry

    lax.fori_loop(0, table_ref.shape[0] // TILE, block, 0)


def adagrad(table, state, grad, low_type):
    return pl.pallas_call(
        adagrad_kernel,
        in_specs=[VMEM] * 3,
        out_specs=[VMEM] * 3,
        out_shape=[
            jax.ShapeDtypeStruct(table.shape, jnp.float32),
            jax.ShapeDtypeStruct(state.shape, jnp.float32),
            jax.ShapeDtypeStruct(table.shape, low_type),
        ],
        cost_estimate=pl.CostEstimate(
            flops=8 * table.size, bytes_accessed=8 * table.size, transcendentals=table.shape[0]
        ),
        compiler_params=GRANT,
        name="adagrad",
    )(table, state, grad)


def per_device(
    src_table, src_state, dst_table, dst_state, rel_table, partners, tiles, tile_rel, counts
):
    reps = lax.axis_size("rep")
    rounds = partners.shape[0]
    src_state = src_state.reshape(-1, TILE)
    dst_state = dst_state.reshape(-1, TILE)
    shard_blocks = dst_table.shape[0] // TILE
    number = reps * shard_blocks
    slots = tiles.shape[-1]
    lists = layout(number, slots)
    none_rel = rel_table.shape[0]
    scalars = (
        lax.axis_index("rep").astype(jnp.int32).reshape(1), tiles[0, 0], tile_rel[0, 0], counts[0, 0],
    )
    plan_shape = jax.ShapeDtypeStruct((1, lists[-1]), jnp.int32)
    plan, rows, *masks = pl.pallas_call(
        functools.partial(first_kernel, rounds, number, none_rel),
        in_specs=[SMEM] * 5 + [VMEM],
        out_specs=[SMEM, VMEM] + [SMEM] * rounds,
        out_shape=[plan_shape, jax.ShapeDtypeStruct(dst_table.shape, jnp.bfloat16)]
        + [jax.ShapeDtypeStruct((1, 1), jnp.int32)] * rounds,
        compiler_params=pltpu.CompilerParams(vmem_limit_bytes=FIRST_GRANT),
        name="first",
    )(*scalars, partners, dst_table)
    for k in range(rounds):
        mask = masks[k].reshape(())
        own = bucket_send(rows, mask)
        others = []
        for j in range(1, reps):
            others.append(rep_send(own, j))
        if k == 0:
            low, rel_rows = round_source(src_table, rel_table)
        src_grad, parts = tile_work(0, lists, slots, plan, low, rel_rows, others, None)
        for j in range(1, reps):
            parts[j - 1] = rep_send(parts[j - 1], j)
        src_grad, mine = tile_work(
            1, lists, slots // reps, plan, low, rel_rows, [own], src_grad
        )
        total = functools.reduce(jnp.add, [x.astype(jnp.float32) for x in mine + parts])
        if k + 1 < rounds:
            plan = pl.pallas_call(
                functools.partial(later_kernel, k + 1, shard_blocks, number, none_rel),
                in_specs=[SMEM] * 4 + [pl.BlockSpec(memory_space=pl.ANY)],
                out_specs=SMEM,
                out_shape=plan_shape,
                compiler_params=GRANT,
                name="later",
            )(*scalars, src_grad)
        src_table, src_state, low = adagrad(src_table, src_state, src_grad, jnp.float32)
        total = bucket_send(total.astype(jnp.bfloat16), mask)
        dst_table, dst_state, rows = adagrad(dst_table, dst_state, total, jnp.bfloat16)
    return (src_table, src_state.reshape(-1), dst_table, dst_state.reshape(-1))


def solution(mesh):
    table, state = P(AXES, None), P(AXES)
    in_specs = (
        table,
        state,
        table,
        state,
        P(),
        P(),
        P("bucket", "rep", None, None),
        P("bucket", "rep", None, None),
        P("bucket", "rep", None),
    )
    return jax.shard_map(
        per_device,
        mesh=mesh,
        in_specs=in_specs,
        out_specs=(table, state, table, state),
        check_vma=False,
    )
```

```python
import functools

import jax
import jax.numpy as jnp
from jax import lax
from jax.experimental import pallas as pl
from jax.experimental.pallas import tpu as pltpu
from jax.sharding import PartitionSpec as P

TILE = 128
GROUP = 4
LOW_BITS = 3
SHIFT = 16

learn_rate = 0.1

AXES = ("bucket", "rep")
SMEM = pl.BlockSpec(memory_space=pltpu.SMEM)
VMEM = pl.BlockSpec(memory_space=pltpu.VMEM)
FIRST_GRANT = 60 * 1024 * 1024
GRANT = pltpu.CompilerParams(vmem_limit_bytes=12 * 1024 * 1024)


def send(rows, bucket_xor, rep_xor):
    if bucket_xor == 0 and rep_xor == 0:
        return rows
    buckets, reps = lax.axis_size("bucket"), lax.axis_size("rep")
    pairs = [
        (b * reps + r, (b ^ bucket_xor) * reps + (r ^ rep_xor))
        for b in range(buckets)
        for r in range(reps)
    ]
    return lax.ppermute(rows, AXES, pairs)


def bit_chunks():
    bits = lax.axis_size("bucket").bit_length() - 1
    return [(at, min(LOW_BITS, bits - at)) for at in range(0, bits, LOW_BITS)]


def by_mask(mask, chunk, branch, operands):
    first, width = chunk
    if (1 << width) == lax.axis_size("bucket"):
        least, index = 1, mask - 1
    else:
        least, index = 0, jnp.bitwise_and(jnp.right_shift(mask, first), (1 << width) - 1)
    branches = [functools.partial(branch, value << first) for value in range(least, 1 << width)]
    return lax.switch(index, branches, operands)


def send_high(rows, mask):
    for chunk in bit_chunks()[1:]:
        rows = by_mask(mask, chunk, lambda value, x: send(x, value, 0), rows)
    return rows


def layout(number, slots):
    most = slots // GROUP + number + 3
    first = 2
    second = first + most
    start = second + most
    room = 1 << (slots + 2 * GROUP - 1).bit_length()
    return first, second, start, room, start + number * room


def sort_tiles(k, cut, none_rel, flip, number, tiles, rel, counts, plan):
    bits = number.bit_length() - 1
    first, second, start, room, _ = layout(number, tiles.shape[1])

    def place(t, ends):
        code = tiles[k, t]
        e = jnp.bitwise_xor(jnp.bitwise_and(code, number - 1), flip)
        p = ends[0]
        for i in range(1, number):
            p = jnp.where(e == i, ends[i], p)
        plan[0, start + e * room + p] = jnp.bitwise_or(
            jnp.left_shift(jnp.right_shift(code, bits), SHIFT), rel[k, t]
        )
        return tuple(ends[i] + jnp.where(e == i, 1, 0) for i in range(number))

    ends = lax.fori_loop(0, counts[k], place, (jnp.int32(0),) * number)
    for i in range(number):
        for extra in range(2 * GROUP):
            plan[0, start + i * room + ends[i] + extra] = jnp.int32(none_rel)
    for index, at, blocks in ((0, first, range(cut)), (1, second, range(cut, number))):
        q = jnp.int32(0)
        for i in blocks:
            amount = jnp.right_shift(ends[i] + (GROUP - 1), GROUP.bit_length() - 1)

            def name(g, carry, i=i, q=q, at=at):
                plan[0, at + q + g] = i * room + g * GROUP
                return carry

            lax.fori_loop(0, amount, name, 0)
            q = q + amount
        plan[0, index] = jnp.right_shift(q + 1, 1)
        for extra in range(3):
            plan[0, at + q + extra] = blocks[0] * room + ends[blocks[0]]


def first_kernel(rounds, number, cut, none_rel, rep, tiles, rel, counts, partners, dst_ref, rel_ref, plan, rows_ref, row_ref, *masks):
    rows_ref[...] = dst_ref[...].astype(jnp.bfloat16)
    row_ref[pl.ds(0, none_rel), :] = rel_ref[...] * (0.5 * rel_ref.shape[1] ** -0.5)
    row_ref[pl.ds(none_rel, 8), :] = jnp.zeros((8, rel_ref.shape[1]), jnp.float32)
    for k in range(rounds):
        masks[k][0, 0] = partners[k, 0]
    flip = rep[0] * (dst_ref.shape[0] // TILE)
    sort_tiles(0, cut, none_rel, flip, number, tiles, rel, counts, plan)


def later_kernel(k, shard_blocks, number, cut, none_rel, rep, tiles, rel, counts, after, plan):
    sort_tiles(k, cut, none_rel, rep[0] * shard_blocks, number, tiles, rel, counts, plan)


def tile_kernel(index, lists, cut, shards, carried, plan, src_ref, row_ref, *refs):
    dst_refs, refs = refs[:shards], refs[shards + carried :]
    src_grad, parts, refs = refs[0], refs[1 : 1 + shards], refs[1 + shards :]
    low_ref, dst_all, dst_grad, held_rows, held_slope = refs
    _, _, start, room, _ = lists
    at_list = lists[index]
    rows_of_shard = dst_refs[0].shape[0]
    first_row = cut * TILE if index == 1 else 0

    def begin(i, carry):
        rows = pl.ds(pl.multiple_of(i * TILE, TILE), TILE)
        low_ref[rows, :] = src_ref[rows, :].astype(jnp.bfloat16).astype(jnp.float32)
        if not carried:
            src_grad[rows, :] = jnp.zeros((TILE, src_grad.shape[1]), jnp.float32)
        return carry

    lax.fori_loop(0, src_ref.shape[0] // TILE, begin, 0)
    for i in range(shards):
        dst_all[pl.ds(i * rows_of_shard, rows_of_shard), :] = dst_refs[i][...]
    dst_grad[...] = jnp.zeros_like(dst_grad)
    row_id = lax.broadcasted_iota(jnp.int32, (TILE, TILE), 0)
    column_id = lax.broadcasted_iota(jnp.int32, (TILE, TILE), 1)
    offset = jnp.where(row_id == column_id, -1.0, 1.0).astype(jnp.float32)
    pairs = plan[0, index]

    def group(q):
        at = plan[0, at_list + q]
        block = jnp.right_shift(at, room.bit_length() - 1)
        where, rows = [], []
        for g in range(GROUP):
            code = plan[0, start + at + g]
            where.append(pl.multiple_of(jnp.right_shift(code, SHIFT) * TILE, TILE))
            rows.append(row_ref[pl.ds(jnp.bitwise_and(code, (1 << SHIFT) - 1), 1), :])
        return pl.ds(pl.multiple_of(block * TILE - first_row, TILE), TILE), where, rows

    def slopes(q, slot):
        dst_rows, where, rows = group(q)
        src_rel = jnp.concatenate(
            [(low_ref[pl.ds(s, TILE), :] * row).astype(jnp.bfloat16) for s, row in zip(where, rows)], 0
        )
        scores = lax.dot_general(
            src_rel, dst_all[dst_rows, :], (((1,), (1,)), ((), ())), preferred_element_type=jnp.float32
        )
        slope = jnp.concatenate(
            [
                (jnp.tanh(scores[g * TILE : (g + 1) * TILE]) + offset).astype(jnp.bfloat16)
                for g in range(GROUP)
            ],
            0,
        )
        held_rows[slot] = src_rel
        held_slope[slot] = slope

    def grads(q, slot):
        dst_rows, where, rows = group(q)
        slope = held_slope[slot]
        src_terms = jnp.dot(slope, dst_all[dst_rows, :], preferred_element_type=jnp.float32)
        dst_grad[dst_rows, :] += lax.dot_general(
            slope, held_rows[slot], (((0,), (0,)), ((), ())), preferred_element_type=jnp.float32
        )
        for g in range(GROUP):
            src_grad[pl.ds(where[g], TILE), :] += src_terms[g * TILE : (g + 1) * TILE] * rows[g]

    @pl.when(pairs > 0)
    def _():
        slopes(0, 0)

        def two(p, carry):
            q = p * 2
            slopes(q + 1, 1)
            grads(q, 0)
            slopes(q + 2, 0)
            grads(q + 1, 1)
            return carry

        lax.fori_loop(0, pairs, two, 0)

    for i in range(shards):
        parts[i][...] = dst_grad[pl.ds(i * rows_of_shard, rows_of_shard), :].astype(jnp.bfloat16)


def tile_work(index, lists, cut, slots, plan, src_table, rel_rows, shards, src_grad):
    rows, width = shards[0].shape
    carried = [] if src_grad is None else [src_grad]
    out = pl.pallas_call(
        functools.partial(tile_kernel, index, lists, cut, len(shards), len(carried)),
        in_specs=[SMEM] + [VMEM] * (2 + len(shards) + len(carried)),
        out_specs=[VMEM] * (1 + len(shards)),
        out_shape=[jax.ShapeDtypeStruct(src_table.shape, jnp.float32)]
        + [jax.ShapeDtypeStruct((rows, width), jnp.bfloat16)] * len(shards),
        scratch_shapes=[
            pltpu.VMEM(src_table.shape, jnp.float32),
            pltpu.VMEM((len(shards) * rows, width), jnp.bfloat16),
            pltpu.VMEM((len(shards) * rows, width), jnp.float32),
            pltpu.VMEM((2, GROUP * TILE, width), jnp.bfloat16),
            pltpu.VMEM((2, GROUP * TILE, TILE), jnp.bfloat16),
        ],
        input_output_aliases={3 + len(shards): 0} if carried else {},
        cost_estimate=pl.CostEstimate(
            flops=6 * slots * TILE * TILE * width,
            bytes_accessed=4 * src_table.size,
            transcendentals=slots * TILE * TILE,
        ),
        compiler_params=GRANT,
        name="tile_work",
    )(plan, src_table, rel_rows, *shards, *carried)
    return out[0], list(out[1:])


def adagrad_block(table, state, grad):
    row_id = lax.broadcasted_iota(jnp.int32, (TILE, TILE), 0)
    column_id = lax.broadcasted_iota(jnp.int32, (TILE, TILE), 1)
    same = row_id == column_id
    state = jnp.sum(jnp.where(same, state, 0.0), axis=1, keepdims=True)
    state = state + jnp.sum(grad * grad, axis=1, keepdims=True) * (1.0 / grad.shape[1])
    table = table - learn_rate * grad / jnp.sqrt(state)
    return table, jnp.sum(jnp.where(same, state, 0.0), axis=0, keepdims=True)


def source_kernel(table_ref, state_ref, grad_ref, table_out, state_out, table_new, state_new, sem):
    blocks = table_ref.shape[0] // TILE

    def block(i, carry):
        rows = pl.ds(pl.multiple_of(i * TILE, TILE), TILE)
        table_new[rows, :], state_new[pl.ds(i, 1), :] = adagrad_block(
            table_ref[rows, :], state_ref[pl.ds(i, 1), :], grad_ref[rows, :]
        )
        return carry

    lax.fori_loop(0, blocks, block, 0)
    copies = [
        pltpu.make_async_copy(table_new, table_out, sem.at[0]),
        pltpu.make_async_copy(state_new, state_out, sem.at[1]),
    ]
    for copy in copies:
        copy.start()
    for copy in copies:
        copy.wait()


def update_source(table, state, grad):
    return pl.pallas_call(
        source_kernel,
        in_specs=[VMEM] * 3,
        out_specs=[pl.BlockSpec(memory_space=pltpu.HBM)] * 2,
        out_shape=[pltpu.HBM(table.shape, jnp.float32), pltpu.HBM(state.shape, jnp.float32)],
        scratch_shapes=[
            pltpu.VMEM(table.shape, jnp.float32),
            pltpu.VMEM(state.shape, jnp.float32),
            pltpu.SemaphoreType.DMA((2,)),
        ],
        cost_estimate=pl.CostEstimate(
            flops=8 * table.size, bytes_accessed=8 * table.size, transcendentals=table.shape[0]
        ),
        compiler_params=GRANT,
        name="update_source",
    )(table, state, grad)


def target_kernel(parts, last, table_ref, state_ref, *refs):
    for i in range(table_ref.shape[0] // TILE):
        rows = pl.ds(i * TILE, TILE)
        grad = refs[0][rows, :].astype(jnp.float32)
        for other in refs[1:parts]:
            grad = grad + other[rows, :].astype(jnp.float32)
        if parts > 1:
            grad = grad.astype(jnp.bfloat16).astype(jnp.float32)
        table, state = adagrad_block(table_ref[rows, :], state_ref[pl.ds(i, 1), :], grad)
        refs[parts][rows, :] = table
        refs[parts + 1][pl.ds(i, 1), :] = state
        if not last:
            refs[parts + 2][rows, :] = table.astype(jnp.bfloat16)


def update_target(table, state, parts, last):
    low = [] if last else [jax.ShapeDtypeStruct(table.shape, jnp.bfloat16)]
    return pl.pallas_call(
        functools.partial(target_kernel, len(parts), last),
        in_specs=[VMEM] * (2 + len(parts)),
        out_specs=[VMEM] * (2 + len(low)),
        out_shape=[
            jax.ShapeDtypeStruct(table.shape, jnp.float32),
            jax.ShapeDtypeStruct(state.shape, jnp.float32),
        ]
        + low,
        cost_estimate=pl.CostEstimate(
            flops=8 * table.size, bytes_accessed=8 * table.size, transcendentals=table.shape[0]
        ),
        compiler_params=GRANT,
        name="update_target",
    )(table, state, *parts)


def per_device(
    src_table, src_state, dst_table, dst_state, rel_table, partners, tiles, tile_rel, counts
):
    reps = lax.axis_size("rep")
    rounds = partners.shape[0]
    src_state = src_state.reshape(-1, TILE)
    dst_state = dst_state.reshape(-1, TILE)
    shard_blocks = dst_table.shape[0] // TILE
    number = reps * shard_blocks
    slots = tiles.shape[-1]
    lists = layout(number, slots)
    none_rel = rel_table.shape[0]
    near = reps // 2
    cut = near * shard_blocks
    low_chunk, *high_chunks = bit_chunks()
    scalars = (
        lax.axis_index("rep").astype(jnp.int32).reshape(1), tiles[0, 0], tile_rel[0, 0], counts[0, 0],
    )
    plan_shape = jax.ShapeDtypeStruct((1, lists[-1]), jnp.int32)
    plan, rows, rel_rows, *masks = pl.pallas_call(
        functools.partial(first_kernel, rounds, number, cut, none_rel),
        in_specs=[SMEM] * 5 + [VMEM] * 2,
        out_specs=[SMEM, VMEM, VMEM] + [SMEM] * rounds,
        out_shape=[
            plan_shape,
            jax.ShapeDtypeStruct(dst_table.shape, jnp.bfloat16),
            jax.ShapeDtypeStruct((none_rel + 8, rel_table.shape[1]), jnp.float32),
        ]
        + [jax.ShapeDtypeStruct((1, 1), jnp.int32)] * rounds,
        compiler_params=pltpu.CompilerParams(vmem_limit_bytes=FIRST_GRANT),
        name="first",
    )(*scalars, partners, dst_table, rel_table)

    def branch(value, operands, k):
        rows, plan, rel_rows, src_table, src_state, scalars = operands
        shards = []
        for j in range(reps):
            shards.append(send(rows, value, j))
        src_grad, parts = tile_work(
            0, lists, cut, slots // 2, plan, src_table, rel_rows, shards[:near], None
        )
        back = []
        for j in range(near):
            back.append(send(parts[j], value, j))
        src_grad, parts = tile_work(1, lists, cut, slots // 2, plan, src_table, rel_rows, shards[near:], src_grad)
        for j in range(near, reps):
            back.append(send(parts[j - near], value, j))
        if k + 1 < rounds:
            plan = pl.pallas_call(
                functools.partial(later_kernel, k + 1, shard_blocks, number, cut, none_rel),
                in_specs=[SMEM] * 4 + [pl.BlockSpec(memory_space=pl.ANY)],
                out_specs=SMEM,
                out_shape=plan_shape,
                compiler_params=GRANT,
                name="later",
            )(*scalars, src_grad)
        src_table, src_state = update_source(src_table, src_state, src_grad)
        return tuple(back), (plan,) if k + 1 < rounds else (), src_table, src_state

    for k in range(rounds):
        mask = masks[k].reshape(())
        back, plans, src_table, src_state = by_mask(
            mask,
            low_chunk,
            functools.partial(branch, k=k),
            (send_high(rows, mask), plan, rel_rows, src_table, src_state, scalars),
        )
        (plan,) = plans or (None,)
        if high_chunks:
            total = functools.reduce(jnp.add, [x.astype(jnp.float32) for x in back])
            back = [send_high(total.astype(jnp.bfloat16), mask)]
        dst_table, dst_state, *rows = update_target(dst_table, dst_state, back, k + 1 == rounds)
        rows = rows[0] if rows else None
    return (src_table, src_state.reshape(-1), dst_table, dst_state.reshape(-1))


def solution(mesh):
    table, state = P(AXES, None), P(AXES)
    in_specs = (
        table,
        state,
        table,
        state,
        P(),
        P(),
        P("bucket", "rep", None, None),
        P("bucket", "rep", None, None),
        P("bucket", "rep", None),
    )
    return jax.shard_map(
        per_device,
        mesh=mesh,
        in_specs=in_specs,
        out_specs=(table, state, table, state),
        check_vma=False,
    )
```

```python
import functools

import jax
import jax.numpy as jnp
from jax import lax
from jax.experimental import pallas as pl
from jax.experimental.pallas import tpu as pltpu
from jax.sharding import PartitionSpec as P

TILE = 128
GROUP = 4
LOW_BITS = 3
SHIFT = 16

learn_rate = 0.1

AXES = ("bucket", "rep")
SMEM = pl.BlockSpec(memory_space=pltpu.SMEM)
VMEM = pl.BlockSpec(memory_space=pltpu.VMEM)
HBM = pl.BlockSpec(memory_space=pltpu.HBM)
GRANT = pltpu.CompilerParams(vmem_limit_bytes=12 * 1024 * 1024)


def send(rows, bucket_xor, rep_xor):
    if bucket_xor == 0 and rep_xor == 0:
        return rows
    buckets, reps = lax.axis_size("bucket"), lax.axis_size("rep")
    pairs = [
        (b * reps + r, (b ^ bucket_xor) * reps + (r ^ rep_xor))
        for b in range(buckets)
        for r in range(reps)
    ]
    return lax.ppermute(rows, AXES, pairs)


def bit_chunks():
    bits = lax.axis_size("bucket").bit_length() - 1
    return [(at, min(LOW_BITS, bits - at)) for at in range(0, bits, LOW_BITS)]


def by_mask(mask, chunk, branch, operands):
    first, width = chunk
    if (1 << width) == lax.axis_size("bucket"):
        least, index = 1, mask - 1
    else:
        least, index = 0, jnp.bitwise_and(jnp.right_shift(mask, first), (1 << width) - 1)
    branches = [functools.partial(branch, value << first) for value in range(least, 1 << width)]
    return lax.switch(index, branches, operands)


def send_high(rows, mask):
    for chunk in bit_chunks()[1:]:
        rows = by_mask(mask, chunk, lambda value, x: send(x, value, 0), rows)
    return rows


def layout(number, slots):
    most = slots // GROUP + number + 3
    first = 2
    second = first + most
    start = second + most
    room = 1 << (slots + 2 * GROUP - 1).bit_length()
    return first, second, start, room, start + number * room


def sort_tiles(k, cut, none_rel, flip, number, tiles, rel, counts, plan):
    bits = number.bit_length() - 1
    first, second, start, room, _ = layout(number, tiles.shape[1])

    def place(t, ends):
        code = tiles[k, t]
        e = jnp.bitwise_xor(jnp.bitwise_and(code, number - 1), flip)
        p = ends[0]
        for i in range(1, number):
            p = jnp.where(e == i, ends[i], p)
        plan[0, start + e * room + p] = jnp.bitwise_or(
            jnp.left_shift(jnp.right_shift(code, bits), SHIFT), rel[k, t]
        )
        return tuple(ends[i] + jnp.where(e == i, 1, 0) for i in range(number))

    ends = lax.fori_loop(0, counts[k], place, (jnp.int32(0),) * number)
    for i in range(number):
        for extra in range(2 * GROUP):
            plan[0, start + i * room + ends[i] + extra] = jnp.int32(none_rel)
    for index, at, blocks in ((0, first, range(cut)), (1, second, range(cut, number))):
        q = jnp.int32(0)
        for i in blocks:
            amount = jnp.right_shift(ends[i] + (GROUP - 1), GROUP.bit_length() - 1)

            def name(g, carry, i=i, q=q, at=at):
                plan[0, at + q + g] = i * room + g * GROUP
                return carry

            lax.fori_loop(0, amount, name, 0)
            q = q + amount
        plan[0, index] = jnp.right_shift(q + 1, 1)
        for extra in range(3):
            plan[0, at + q + extra] = blocks[0] * room + ends[blocks[0]]


def in_hbm(*arrays):
    return [pltpu.with_memory_space_constraint(array, pltpu.HBM) for array in arrays]


def fetch(sources, targets, sem):
    copies = [
        pltpu.make_async_copy(source, target, sem.at[i])
        for i, (source, target) in enumerate(zip(sources, targets))
    ]
    for copy in copies:
        copy.start()
    return copies


def first_kernel(number, cut, none_rel, rep, *refs):
    sources, (plan, rows_ref, row_ref, mask), held, sem = refs[:6], refs[6:10], refs[10:16], refs[16]
    copies = fetch(sources, held, sem)
    tiles, rel, counts, partners, dst_ref, rel_ref = held
    for copy in copies:
        copy.wait()
    rows_ref[...] = dst_ref[...].astype(jnp.bfloat16)
    row_ref[pl.ds(0, none_rel), :] = rel_ref[...] * (0.5 * rel_ref.shape[1] ** -0.5)
    row_ref[pl.ds(none_rel, 8), :] = jnp.zeros((8, rel_ref.shape[1]), jnp.float32)
    mask[0, 0] = partners[0, 0]
    flip = rep[0] * (dst_ref.shape[0] // TILE)
    sort_tiles(0, cut, none_rel, flip, number, tiles, rel, counts, plan)


def later_kernel(k, shard_blocks, number, cut, none_rel, rep, *refs):
    sources, (plan, mask), held, sem = refs[:4], refs[5:7], refs[7:11], refs[11]
    for copy in fetch(sources, held, sem):
        copy.wait()
    tiles, rel, counts, partners = held
    mask[0, 0] = partners[k, 0]
    sort_tiles(k, cut, none_rel, rep[0] * shard_blocks, number, tiles, rel, counts, plan)


def tile_kernel(index, lists, cut, shards, carried, plan, src_ref, row_ref, *refs):
    dst_refs, refs = refs[:shards], refs[shards + carried :]
    src_grad, parts, refs = refs[0], refs[1 : 1 + shards], refs[1 + shards :]
    low_ref, dst_all, dst_grad, held_rows, held_slope = refs
    _, _, start, room, _ = lists
    at_list = lists[index]
    rows_of_shard = dst_refs[0].shape[0]
    first_row = cut * TILE if index == 1 else 0

    def begin(i, carry):
        rows = pl.ds(pl.multiple_of(i * TILE, TILE), TILE)
        low_ref[rows, :] = src_ref[rows, :].astype(jnp.bfloat16).astype(jnp.float32)
        if not carried:
            src_grad[rows, :] = jnp.zeros((TILE, src_grad.shape[1]), jnp.float32)
        return carry

    lax.fori_loop(0, src_ref.shape[0] // TILE, begin, 0)
    for i in range(shards):
        dst_all[pl.ds(i * rows_of_shard, rows_of_shard), :] = dst_refs[i][...]
    dst_grad[...] = jnp.zeros_like(dst_grad)
    row_id = lax.broadcasted_iota(jnp.int32, (TILE, TILE), 0)
    column_id = lax.broadcasted_iota(jnp.int32, (TILE, TILE), 1)
    offset = jnp.where(row_id == column_id, -1.0, 1.0).astype(jnp.float32)
    pairs = plan[0, index]

    def group(q):
        at = plan[0, at_list + q]
        block = jnp.right_shift(at, room.bit_length() - 1)
        where, rows = [], []
        for g in range(GROUP):
            code = plan[0, start + at + g]
            where.append(pl.multiple_of(jnp.right_shift(code, SHIFT) * TILE, TILE))
            rows.append(row_ref[pl.ds(jnp.bitwise_and(code, (1 << SHIFT) - 1), 1), :])
        return pl.ds(pl.multiple_of(block * TILE - first_row, TILE), TILE), where, rows

    def slopes(q, slot):
        dst_rows, where, rows = group(q)
        src_rel = jnp.concatenate(
            [(low_ref[pl.ds(s, TILE), :] * row).astype(jnp.bfloat16) for s, row in zip(where, rows)], 0
        )
        scores = lax.dot_general(
            src_rel, dst_all[dst_rows, :], (((1,), (1,)), ((), ())), preferred_element_type=jnp.float32
        )
        slope = jnp.concatenate(
            [
                (jnp.tanh(scores[g * TILE : (g + 1) * TILE]) + offset).astype(jnp.bfloat16)
                for g in range(GROUP)
            ],
            0,
        )
        held_rows[slot] = src_rel
        held_slope[slot] = slope

    def grads(q, slot):
        dst_rows, where, rows = group(q)
        slope = held_slope[slot]
        src_terms = jnp.dot(slope, dst_all[dst_rows, :], preferred_element_type=jnp.float32)
        dst_grad[dst_rows, :] += lax.dot_general(
            slope, held_rows[slot], (((0,), (0,)), ((), ())), preferred_element_type=jnp.float32
        )
        for g in range(GROUP):
            src_grad[pl.ds(where[g], TILE), :] += src_terms[g * TILE : (g + 1) * TILE] * rows[g]

    @pl.when(pairs > 0)
    def _():
        slopes(0, 0)

        def two(p, carry):
            q = p * 2
            slopes(q + 1, 1)
            grads(q, 0)
            slopes(q + 2, 0)
            grads(q + 1, 1)
            return carry

        lax.fori_loop(0, pairs, two, 0)

    for i in range(shards):
        parts[i][...] = dst_grad[pl.ds(i * rows_of_shard, rows_of_shard), :].astype(jnp.bfloat16)


def tile_work(index, lists, cut, slots, plan, src_table, rel_rows, shards, src_grad):
    rows, width = shards[0].shape
    carried = [] if src_grad is None else [src_grad]
    out = pl.pallas_call(
        functools.partial(tile_kernel, index, lists, cut, len(shards), len(carried)),
        in_specs=[SMEM] + [VMEM] * (2 + len(shards) + len(carried)),
        out_specs=[VMEM] * (1 + len(shards)),
        out_shape=[jax.ShapeDtypeStruct(src_table.shape, jnp.float32)]
        + [jax.ShapeDtypeStruct((rows, width), jnp.bfloat16)] * len(shards),
        scratch_shapes=[
            pltpu.VMEM(src_table.shape, jnp.float32),
            pltpu.VMEM((len(shards) * rows, width), jnp.bfloat16),
            pltpu.VMEM((len(shards) * rows, width), jnp.float32),
            pltpu.VMEM((2, GROUP * TILE, width), jnp.bfloat16),
            pltpu.VMEM((2, GROUP * TILE, TILE), jnp.bfloat16),
        ],
        input_output_aliases={3 + len(shards): 0} if carried else {},
        cost_estimate=pl.CostEstimate(
            flops=6 * slots * TILE * TILE * width,
            bytes_accessed=4 * src_table.size,
            transcendentals=slots * TILE * TILE,
        ),
        compiler_params=GRANT,
        name="tile_work",
    )(plan, src_table, rel_rows, *shards, *carried)
    return out[0], list(out[1:])


def adagrad_block(table, state, grad):
    row_id = lax.broadcasted_iota(jnp.int32, (TILE, TILE), 0)
    column_id = lax.broadcasted_iota(jnp.int32, (TILE, TILE), 1)
    same = row_id == column_id
    state = jnp.sum(jnp.where(same, state, 0.0), axis=1, keepdims=True)
    state = state + jnp.sum(grad * grad, axis=1, keepdims=True) * (1.0 / grad.shape[1])
    table = table - learn_rate * grad / jnp.sqrt(state)
    return table, jnp.sum(jnp.where(same, state, 0.0), axis=0, keepdims=True)


def source_kernel(table_ref, state_hbm, grad_ref, table_out, state_out, table_new, state_new, state_ref, sem):
    blocks = table_ref.shape[0] // TILE
    (state_in,) = fetch([state_hbm], [state_ref], sem)
    state_in.wait()

    def block(i, carry):
        rows = pl.ds(pl.multiple_of(i * TILE, TILE), TILE)
        table_new[rows, :], state_new[pl.ds(i, 1), :] = adagrad_block(
            table_ref[rows, :], state_ref[pl.ds(i, 1), :], grad_ref[rows, :]
        )
        return carry

    lax.fori_loop(0, blocks, block, 0)
    for copy in fetch([table_new, state_new], [table_out, state_out], sem):
        copy.wait()


def update_source(table, state, grad):
    return pl.pallas_call(
        source_kernel,
        in_specs=[VMEM, HBM, VMEM],
        out_specs=[HBM] * 2,
        out_shape=[pltpu.HBM(table.shape, jnp.float32), pltpu.HBM(state.shape, jnp.float32)],
        scratch_shapes=[
            pltpu.VMEM(table.shape, jnp.float32),
            pltpu.VMEM(state.shape, jnp.float32),
            pltpu.VMEM(state.shape, jnp.float32),
            pltpu.SemaphoreType.DMA((2,)),
        ],
        cost_estimate=pl.CostEstimate(
            flops=8 * table.size, bytes_accessed=8 * table.size, transcendentals=table.shape[0]
        ),
        compiler_params=GRANT,
        name="update_source",
    )(table, *in_hbm(state), grad)


def target_kernel(parts, last, table_ref, *refs):
    sources, outs = refs[: parts + 1], refs[parts + 1 : parts + 3 + (not last)]
    *held, sem = refs[parts + 3 + (not last) :]
    for copy in fetch(sources, held, sem):
        copy.wait()
    for i in range(table_ref.shape[0] // TILE):
        rows = pl.ds(i * TILE, TILE)
        grad = held[1][rows, :].astype(jnp.float32)
        for other in held[2:]:
            grad = grad + other[rows, :].astype(jnp.float32)
        if parts > 1:
            grad = grad.astype(jnp.bfloat16).astype(jnp.float32)
        table, state = adagrad_block(table_ref[rows, :], held[0][pl.ds(i, 1), :], grad)
        outs[0][rows, :] = table
        outs[1][pl.ds(i, 1), :] = state
        if not last:
            outs[2][rows, :] = table.astype(jnp.bfloat16)


def update_target(table, state, parts, first, last):
    low = [] if last else [jax.ShapeDtypeStruct(table.shape, jnp.bfloat16)]
    return pl.pallas_call(
        functools.partial(target_kernel, len(parts), last),
        in_specs=[VMEM] + [HBM] * (1 + len(parts)),
        out_specs=[VMEM] * (2 + len(low)),
        scratch_shapes=[pltpu.VMEM(state.shape, jnp.float32)]
        + [pltpu.VMEM(part.shape, part.dtype) for part in parts]
        + [pltpu.SemaphoreType.DMA((1 + len(parts),))],
        out_shape=[
            jax.ShapeDtypeStruct(table.shape, jnp.float32),
            jax.ShapeDtypeStruct(state.shape, jnp.float32),
        ]
        + low,
        cost_estimate=pl.CostEstimate(
            flops=8 * table.size, bytes_accessed=8 * table.size, transcendentals=table.shape[0]
        ),
        compiler_params=GRANT,
        name="update_target",
    )(table, *(in_hbm(state) if first else [state]), *parts)


def per_device(
    src_table, src_state, dst_table, dst_state, rel_table, partners, tiles, tile_rel, counts
):
    reps = lax.axis_size("rep")
    rounds = partners.shape[0]
    src_state = src_state.reshape(-1, TILE)
    dst_state = dst_state.reshape(-1, TILE)
    shard_blocks = dst_table.shape[0] // TILE
    number = reps * shard_blocks
    slots = tiles.shape[-1]
    lists = layout(number, slots)
    none_rel = rel_table.shape[0]
    near = reps // 2
    cut = near * shard_blocks
    low_chunk, *high_chunks = bit_chunks()
    scalars = (
        lax.axis_index("rep").astype(jnp.int32).reshape(1), tiles[0, 0], tile_rel[0, 0], counts[0, 0], partners,
    )
    held = [pltpu.SMEM(x.shape, jnp.int32) for x in scalars[1:]]
    mask_shape = jax.ShapeDtypeStruct((1, 1), jnp.int32)
    plan_shape = jax.ShapeDtypeStruct((1, lists[-1]), jnp.int32)
    plan, rows, rel_rows, mask = pl.pallas_call(
        functools.partial(first_kernel, number, cut, none_rel),
        in_specs=[SMEM] + [HBM] * 6,
        out_specs=[SMEM, VMEM, VMEM, SMEM],
        out_shape=[
            plan_shape,
            jax.ShapeDtypeStruct(dst_table.shape, jnp.bfloat16),
            jax.ShapeDtypeStruct((none_rel + 8, rel_table.shape[1]), jnp.float32),
            mask_shape,
        ],
        scratch_shapes=held
        + [
            pltpu.VMEM(dst_table.shape, jnp.float32),
            pltpu.VMEM(rel_table.shape, jnp.float32),
            pltpu.SemaphoreType.DMA((6,)),
        ],
        compiler_params=GRANT,
        name="first",
    )(scalars[0], *in_hbm(*scalars[1:], dst_table, rel_table))

    def branch(value, operands, k):
        rows, plan, rel_rows, src_table, src_state, scalars = operands
        shards = []
        for j in range(reps):
            shards.append(send(rows, value, j))
        src_grad, parts = tile_work(
            0, lists, cut, slots // 2, plan, src_table, rel_rows, shards[:near], None
        )
        back = []
        for j in range(near):
            back.append(send(parts[j], value, j))
        src_grad, parts = tile_work(1, lists, cut, slots // 2, plan, src_table, rel_rows, shards[near:], src_grad)
        for j in range(near, reps):
            back.append(send(parts[j - near], value, j))
        following = ()
        if k + 1 < rounds:
            following = pl.pallas_call(
                functools.partial(later_kernel, k + 1, shard_blocks, number, cut, none_rel),
                in_specs=[SMEM] + [HBM] * 4 + [pl.BlockSpec(memory_space=pl.ANY)],
                out_specs=[SMEM] * 2,
                out_shape=[plan_shape, mask_shape],
                scratch_shapes=held + [pltpu.SemaphoreType.DMA((4,))],
                compiler_params=GRANT,
                name="later",
            )(scalars[0], *in_hbm(*scalars[1:]), src_grad)
        src_table, src_state = update_source(src_table, src_state, src_grad)
        return tuple(back), tuple(following), src_table, src_state

    for k in range(rounds):
        round_mask = mask.reshape(())
        back, following, src_table, src_state = by_mask(
            round_mask,
            low_chunk,
            functools.partial(branch, k=k),
            (send_high(rows, round_mask), plan, rel_rows, src_table, src_state, scalars),
        )
        plan, mask = following or (None, None)
        if high_chunks:
            total = functools.reduce(jnp.add, [x.astype(jnp.float32) for x in back])
            back = [send_high(total.astype(jnp.bfloat16), round_mask)]
        dst_table, dst_state, *rows = update_target(
            dst_table, dst_state, back, k == 0, k + 1 == rounds
        )
        rows = rows[0] if rows else None
    return (src_table, src_state.reshape(-1), dst_table, dst_state.reshape(-1))


def solution(mesh):
    table, state = P(AXES, None), P(AXES)
    in_specs = (
        table,
        state,
        table,
        state,
        P(),
        P(),
        P("bucket", "rep", None, None),
        P("bucket", "rep", None, None),
        P("bucket", "rep", None),
    )
    return jax.shard_map(
        per_device,
        mesh=mesh,
        in_specs=in_specs,
        out_specs=(table, state, table, state),
        check_vma=False,
    )
```

```python
import functools

import jax
import jax.numpy as jnp
from jax import lax
from jax.experimental import pallas as pl
from jax.experimental.pallas import tpu as pltpu
from jax.sharding import PartitionSpec as P

TILE = 128
GROUP = 4
LOW_BITS = 3
SHIFT = 16

learn_rate = 0.1

AXES = ("bucket", "rep")
SMEM = pl.BlockSpec(memory_space=pltpu.SMEM)
VMEM = pl.BlockSpec(memory_space=pltpu.VMEM)
HBM = pl.BlockSpec(memory_space=pltpu.HBM)
GRANT = pltpu.CompilerParams(vmem_limit_bytes=12 * 1024 * 1024)


def send(rows, bucket_xor, rep_xor):
    if bucket_xor == 0 and rep_xor == 0:
        return rows
    buckets, reps = lax.axis_size("bucket"), lax.axis_size("rep")
    pairs = [
        (b * reps + r, (b ^ bucket_xor) * reps + (r ^ rep_xor))
        for b in range(buckets)
        for r in range(reps)
    ]
    return lax.ppermute(rows, AXES, pairs)


def bit_chunks():
    bits = lax.axis_size("bucket").bit_length() - 1
    return [(at, min(LOW_BITS, bits - at)) for at in range(0, bits, LOW_BITS)]


def by_mask(mask, chunk, branch, operands):
    first, width = chunk
    if (1 << width) == lax.axis_size("bucket"):
        least, index = 1, mask - 1
    else:
        least, index = 0, jnp.bitwise_and(jnp.right_shift(mask, first), (1 << width) - 1)
    branches = [functools.partial(branch, value << first) for value in range(least, 1 << width)]
    return lax.switch(index, branches, operands)


def send_high(rows, mask):
    for chunk in bit_chunks()[1:]:
        rows = by_mask(mask, chunk, lambda value, x: send(x, value, 0), rows)
    return rows


def layout(number, slots):
    most = slots // GROUP + number + 3
    first = 2
    second = first + most
    start = second + most
    room = 1 << (slots + 2 * GROUP - 1).bit_length()
    return first, second, start, room, start + number * room


def sort_tiles(k, cut, none_rel, flip, number, tiles, rel, counts, plan):
    bits = number.bit_length() - 1
    first, second, start, room, _ = layout(number, tiles.shape[1])

    live, slots = counts[k], tiles.shape[1]
    some = next(n for n in (4, 2, 1) if slots % n == 0)

    def place(q, ends):
        for u in range(some):
            t = q * some + u
            code = tiles[k, t]
            e = jnp.bitwise_xor(jnp.bitwise_and(code, number - 1), flip)
            p = ends[0]
            for i in range(1, number):
                p = jnp.where(e == i, ends[i], p)
            plan[0, start + e * room + p] = jnp.bitwise_or(
                jnp.left_shift(jnp.right_shift(code, bits), SHIFT), rel[k, t]
            )
            e = jnp.where(t < live, e, number)
            ends = tuple(ends[i] + jnp.where(e == i, 1, 0) for i in range(number))
        return ends

    ends = lax.fori_loop(0, (live + (some - 1)) // some, place, (jnp.int32(0),) * number)
    for i in range(number):
        for extra in range(2 * GROUP):
            plan[0, start + i * room + ends[i] + extra] = jnp.int32(none_rel)
    for index, at, blocks in ((0, first, range(cut)), (1, second, range(cut, number))):
        q = jnp.int32(0)
        for i in blocks:
            amount = jnp.right_shift(ends[i] + (GROUP - 1), GROUP.bit_length() - 1)

            def name(g, carry, i=i, q=q, at=at):
                plan[0, at + q + g] = i * room + g * GROUP
                return carry

            lax.fori_loop(0, amount, name, 0)
            q = q + amount
        plan[0, index] = jnp.right_shift(q + 1, 1)
        for extra in range(3):
            plan[0, at + q + extra] = blocks[0] * room + ends[blocks[0]]


def in_hbm(*arrays):
    return [pltpu.with_memory_space_constraint(array, pltpu.HBM) for array in arrays]


def fetch(sources, targets, sem):
    copies = [
        pltpu.make_async_copy(source, target, sem.at[i])
        for i, (source, target) in enumerate(zip(sources, targets))
    ]
    for copy in copies:
        copy.start()
    return copies


def first_kernel(number, cut, none_rel, rep, *refs):
    sources, (plan, rows_ref, row_ref, mask), held, sem = refs[:6], refs[6:10], refs[10:16], refs[16]
    copies = fetch(sources, held, sem)
    tiles, rel, counts, partners, dst_ref, rel_ref = held
    for copy in copies:
        copy.wait()
    rows_ref[...] = dst_ref[...].astype(jnp.bfloat16)
    row_ref[pl.ds(0, none_rel), :] = rel_ref[...] * (0.5 * rel_ref.shape[1] ** -0.5)
    row_ref[pl.ds(none_rel, 8), :] = jnp.zeros((8, rel_ref.shape[1]), jnp.float32)
    mask[0, 0] = partners[0, 0]
    flip = rep[0] * (dst_ref.shape[0] // TILE)
    sort_tiles(0, cut, none_rel, flip, number, tiles, rel, counts, plan)


def later_kernel(k, shard_blocks, number, cut, none_rel, rep, *refs):
    sources, (plan, mask), held, sem = refs[:4], refs[5:7], refs[7:11], refs[11]
    for copy in fetch(sources, held, sem):
        copy.wait()
    tiles, rel, counts, partners = held
    mask[0, 0] = partners[k, 0]
    sort_tiles(k, cut, none_rel, rep[0] * shard_blocks, number, tiles, rel, counts, plan)


def tile_kernel(index, lists, cut, shards, carried, plan, src_ref, row_ref, *refs):
    dst_refs, refs = refs[:shards], refs[shards + carried :]
    src_grad, parts, refs = refs[0], refs[1 : 1 + shards], refs[1 + shards :]
    *low_out, dst_all, dst_grad, held_rows, held_slope = refs
    (low_ref,) = low_out or (src_ref,)
    _, _, start, room, _ = lists
    at_list = lists[index]
    rows_of_shard = dst_refs[0].shape[0]
    first_row = cut * TILE if index == 1 else 0

    def begin(i, carry):
        rows = pl.ds(pl.multiple_of(i * TILE, TILE), TILE)
        low_ref[rows, :] = src_ref[rows, :].astype(jnp.bfloat16).astype(jnp.float32)
        src_grad[rows, :] = jnp.zeros((TILE, src_grad.shape[1]), jnp.float32)
        return carry

    if not carried:
        lax.fori_loop(0, src_ref.shape[0] // TILE, begin, 0)
    for i in range(shards):
        dst_all[pl.ds(i * rows_of_shard, rows_of_shard), :] = dst_refs[i][...]
    dst_grad[...] = jnp.zeros_like(dst_grad)
    row_id = lax.broadcasted_iota(jnp.int32, (TILE, TILE), 0)
    column_id = lax.broadcasted_iota(jnp.int32, (TILE, TILE), 1)
    offset = jnp.where(row_id == column_id, -1.0, 1.0).astype(jnp.float32)
    pairs = plan[0, index]

    def group(q):
        at = plan[0, at_list + q]
        block = jnp.right_shift(at, room.bit_length() - 1)
        where, rows = [], []
        for g in range(GROUP):
            code = plan[0, start + at + g]
            where.append(pl.multiple_of(jnp.right_shift(code, SHIFT) * TILE, TILE))
            rows.append(row_ref[pl.ds(jnp.bitwise_and(code, (1 << SHIFT) - 1), 1), :])
        return pl.ds(pl.multiple_of(block * TILE - first_row, TILE), TILE), where, rows

    def slopes(q, slot):
        dst_rows, where, rows = group(q)
        src_rel = jnp.concatenate(
            [(low_ref[pl.ds(s, TILE), :] * row).astype(jnp.bfloat16) for s, row in zip(where, rows)], 0
        )
        scores = lax.dot_general(
            src_rel, dst_all[dst_rows, :], (((1,), (1,)), ((), ())), preferred_element_type=jnp.float32
        )
        slope = jnp.concatenate(
            [
                (jnp.tanh(scores[g * TILE : (g + 1) * TILE]) + offset).astype(jnp.bfloat16)
                for g in range(GROUP)
            ],
            0,
        )
        held_rows[slot] = src_rel
        held_slope[slot] = slope

    def grads(q, slot):
        dst_rows, where, rows = group(q)
        slope = held_slope[slot]
        src_terms = jnp.dot(slope, dst_all[dst_rows, :], preferred_element_type=jnp.float32)
        dst_grad[dst_rows, :] += lax.dot_general(
            slope, held_rows[slot], (((0,), (0,)), ((), ())), preferred_element_type=jnp.float32
        )
        for g in range(GROUP):
            src_grad[pl.ds(where[g], TILE), :] += src_terms[g * TILE : (g + 1) * TILE] * rows[g]

    @pl.when(pairs > 0)
    def _():
        slopes(0, 0)

        def two(p, carry):
            q = p * 2
            slopes(q + 1, 1)
            grads(q, 0)
            slopes(q + 2, 0)
            grads(q + 1, 1)
            return carry

        lax.fori_loop(0, pairs, two, 0)

    for i in range(shards):
        parts[i][...] = dst_grad[pl.ds(i * rows_of_shard, rows_of_shard), :].astype(jnp.bfloat16)


def tile_work(index, lists, cut, slots, plan, src_table, rel_rows, shards, src_grad):
    rows, width = shards[0].shape
    carried = [] if src_grad is None else [src_grad]
    out = pl.pallas_call(
        functools.partial(tile_kernel, index, lists, cut, len(shards), len(carried)),
        in_specs=[SMEM] + [VMEM] * (2 + len(shards) + len(carried)),
        out_specs=[VMEM] * (1 + len(shards) + (not carried)),
        out_shape=[jax.ShapeDtypeStruct(src_table.shape, jnp.float32)]
        + [jax.ShapeDtypeStruct((rows, width), jnp.bfloat16)] * len(shards)
        + [jax.ShapeDtypeStruct(src_table.shape, jnp.float32)] * (not carried),
        scratch_shapes=[
            pltpu.VMEM((len(shards) * rows, width), jnp.bfloat16),
            pltpu.VMEM((len(shards) * rows, width), jnp.float32),
            pltpu.VMEM((2, GROUP * TILE, width), jnp.bfloat16),
            pltpu.VMEM((2, GROUP * TILE, TILE), jnp.bfloat16),
        ],
        input_output_aliases={3 + len(shards): 0} if carried else {},
        cost_estimate=pl.CostEstimate(
            flops=6 * slots * TILE * TILE * width,
            bytes_accessed=4 * src_table.size,
            transcendentals=slots * TILE * TILE,
        ),
        compiler_params=GRANT,
        name="tile_work",
    )(plan, src_table, rel_rows, *shards, *carried)
    return out[0], list(out[1 : 1 + len(shards)]), out[-1]


def adagrad_block(table, state, grad):
    row_id = lax.broadcasted_iota(jnp.int32, (TILE, TILE), 0)
    column_id = lax.broadcasted_iota(jnp.int32, (TILE, TILE), 1)
    same = row_id == column_id
    state = jnp.sum(jnp.where(same, state, 0.0), axis=1, keepdims=True)
    state = state + jnp.sum(grad * grad, axis=1, keepdims=True) * (1.0 / grad.shape[1])
    table = table - learn_rate * grad / jnp.sqrt(state)
    return table, jnp.sum(jnp.where(same, state, 0.0), axis=0, keepdims=True)


def source_kernel(table_ref, state_hbm, grad_ref, table_out, state_out, table_new, state_new, state_ref, sem):
    blocks = table_ref.shape[0] // TILE
    (state_in,) = fetch([state_hbm], [state_ref], sem)
    state_in.wait()

    def block(i, carry):
        rows = pl.ds(pl.multiple_of(i * TILE, TILE), TILE)
        table_new[rows, :], state_new[pl.ds(i, 1), :] = adagrad_block(
            table_ref[rows, :], state_ref[pl.ds(i, 1), :], grad_ref[rows, :]
        )
        return carry

    lax.fori_loop(0, blocks, block, 0)
    for copy in fetch([table_new, state_new], [table_out, state_out], sem):
        copy.wait()


def update_source(table, state, grad):
    return pl.pallas_call(
        source_kernel,
        in_specs=[VMEM, HBM, VMEM],
        out_specs=[HBM] * 2,
        out_shape=[pltpu.HBM(table.shape, jnp.float32), pltpu.HBM(state.shape, jnp.float32)],
        scratch_shapes=[
            pltpu.VMEM(table.shape, jnp.float32),
            pltpu.VMEM(state.shape, jnp.float32),
            pltpu.VMEM(state.shape, jnp.float32),
            pltpu.SemaphoreType.DMA((2,)),
        ],
        cost_estimate=pl.CostEstimate(
            flops=8 * table.size, bytes_accessed=8 * table.size, transcendentals=table.shape[0]
        ),
        compiler_params=GRANT,
        name="update_source",
    )(table, *in_hbm(state), grad)


def target_kernel(parts, last, inside, table_ref, *refs):
    sources, outs = refs[: parts + 1], refs[parts + 1 : parts + 3 + (not last)]
    if inside:
        held = sources
    else:
        *held, sem = refs[parts + 3 + (not last) :]
        for copy in fetch(sources, held, sem):
            copy.wait()
    for i in range(table_ref.shape[0] // TILE):
        rows = pl.ds(i * TILE, TILE)
        grad = held[1][rows, :].astype(jnp.float32)
        for other in held[2:]:
            grad = grad + other[rows, :].astype(jnp.float32)
        if parts > 1:
            grad = grad.astype(jnp.bfloat16).astype(jnp.float32)
        table, state = adagrad_block(table_ref[rows, :], held[0][pl.ds(i, 1), :], grad)
        outs[0][rows, :] = table
        outs[1][pl.ds(i, 1), :] = state
        if not last:
            outs[2][rows, :] = table.astype(jnp.bfloat16)


def update_target(table, state, parts, first, last, inside):
    low = [] if last else [jax.ShapeDtypeStruct(table.shape, jnp.bfloat16)]
    return pl.pallas_call(
        functools.partial(target_kernel, len(parts), last, inside),
        in_specs=[VMEM] + [VMEM if inside else HBM] * (1 + len(parts)),
        out_specs=[VMEM] * (2 + len(low)),
        scratch_shapes=[]
        if inside
        else [pltpu.VMEM(state.shape, jnp.float32)]
        + [pltpu.VMEM(part.shape, part.dtype) for part in parts]
        + [pltpu.SemaphoreType.DMA((1 + len(parts),))],
        out_shape=[
            jax.ShapeDtypeStruct(table.shape, jnp.float32),
            jax.ShapeDtypeStruct(state.shape, jnp.float32),
        ]
        + low,
        cost_estimate=pl.CostEstimate(
            flops=8 * table.size, bytes_accessed=8 * table.size, transcendentals=table.shape[0]
        ),
        compiler_params=GRANT,
        name="update_target",
    )(table, *(in_hbm(state) if first and not inside else [state]), *parts)


def per_device(
    src_table, src_state, dst_table, dst_state, rel_table, partners, tiles, tile_rel, counts
):
    reps = lax.axis_size("rep")
    rounds = partners.shape[0]
    src_state = src_state.reshape(-1, TILE)
    dst_state = dst_state.reshape(-1, TILE)
    shard_blocks = dst_table.shape[0] // TILE
    number = reps * shard_blocks
    slots = tiles.shape[-1]
    lists = layout(number, slots)
    none_rel = rel_table.shape[0]
    near = reps // 2
    cut = near * shard_blocks
    low_chunk, *high_chunks = bit_chunks()
    scalars = (
        lax.axis_index("rep").astype(jnp.int32).reshape(1), tiles[0, 0], tile_rel[0, 0], counts[0, 0], partners,
    )
    held = [pltpu.SMEM(x.shape, jnp.int32) for x in scalars[1:]]
    mask_shape = jax.ShapeDtypeStruct((1, 1), jnp.int32)
    plan_shape = jax.ShapeDtypeStruct((1, lists[-1]), jnp.int32)
    plan, rows, rel_rows, mask = pl.pallas_call(
        functools.partial(first_kernel, number, cut, none_rel),
        in_specs=[SMEM] + [HBM] * 6,
        out_specs=[SMEM, VMEM, VMEM, SMEM],
        out_shape=[
            plan_shape,
            jax.ShapeDtypeStruct(dst_table.shape, jnp.bfloat16),
            jax.ShapeDtypeStruct((none_rel + 8, rel_table.shape[1]), jnp.float32),
            mask_shape,
        ],
        scratch_shapes=held
        + [
            pltpu.VMEM(dst_table.shape, jnp.float32),
            pltpu.VMEM(rel_table.shape, jnp.float32),
            pltpu.SemaphoreType.DMA((6,)),
        ],
        compiler_params=GRANT,
        name="first",
    )(scalars[0], *in_hbm(*scalars[1:], dst_table, rel_table))

    def branch(value, operands, k):
        rows, plan, rel_rows, src_table, src_state, scalars, target = operands
        shards = []
        for j in range(reps):
            shards.append(send(rows, value, j))
        src_grad, parts, low = tile_work(0, lists, cut, slots // 2, plan, src_table, rel_rows, shards[:near], None)
        back = []
        for j in range(near):
            back.append(send(parts[j], value, j))
        src_grad, parts, _ = tile_work(
            1, lists, cut, slots // 2, plan, low, rel_rows, shards[near:], src_grad
        )
        for j in range(near, reps):
            back.append(send(parts[j - near], value, j))
        following = ()
        if k + 1 < rounds:
            following = pl.pallas_call(
                functools.partial(later_kernel, k + 1, shard_blocks, number, cut, none_rel),
                in_specs=[SMEM] + [HBM] * 4 + [pl.BlockSpec(memory_space=pl.ANY)],
                out_specs=[SMEM] * 2,
                out_shape=[plan_shape, mask_shape],
                scratch_shapes=held + [pltpu.SemaphoreType.DMA((4,))],
                compiler_params=GRANT,
                name="later",
            )(scalars[0], *in_hbm(*scalars[1:]), src_grad)
        src_table, src_state = update_source(src_table, src_state, src_grad)
        if target:
            back = update_target(*target, back, k == 0, True, True)
        return tuple(back), tuple(following), src_table, src_state

    for k in range(rounds):
        round_mask = mask.reshape(())
        inside = k + 1 == rounds and not high_chunks
        back, following, src_table, src_state = by_mask(
            round_mask,
            low_chunk,
            functools.partial(branch, k=k),
            (
                send_high(rows, round_mask), plan, rel_rows, src_table, src_state, scalars,
                (dst_table, dst_state) if inside else (),
            ),
        )
        plan, mask = following or (None, None)
        if inside:
            dst_table, dst_state = back
            break
        if high_chunks:
            total = functools.reduce(jnp.add, [x.astype(jnp.float32) for x in back])
            back = [send_high(total.astype(jnp.bfloat16), round_mask)]
        dst_table, dst_state, *rows = update_target(
            dst_table, dst_state, back, k == 0, k + 1 == rounds, False
        )
        rows = rows[0] if rows else None
    return (src_table, src_state.reshape(-1), dst_table, dst_state.reshape(-1))


def solution(mesh):
    table, state = P(AXES, None), P(AXES)
    in_specs = (
        table,
        state,
        table,
        state,
        P(),
        P(),
        P("bucket", "rep", None, None),
        P("bucket", "rep", None, None),
        P("bucket", "rep", None),
    )
    return jax.shard_map(
        per_device,
        mesh=mesh,
        in_specs=in_specs,
        out_specs=(table, state, table, state),
        check_vma=False,
    )
```
